32 devices in a mesh: dp: 4 (over z), seq: 8 (over y, x, core).
Axes of the slice: x: 2, y: 2, z: 4, core: 2. Of those that a mesh axis runs over, the one named last changes fastest.
Arguments:
- signal: bfloat16 [8, 1024, 1536], P('dp', 'seq'), may hold values from -6 to 6
- dilated_tap_weight: bfloat16 [3, 1536, 768], P(None, 'dp'), may hold values from -0.09375 to 0.09375
- out_weight: bfloat16 [768, 1536], P(None, 'dp'), may hold values from -0.21875 to 0.21875
- cotangent: bfloat16 [8, 1024, 1536], P('dp', 'seq'), may hold values from -6 to 6
Outputs:
- result: bfloat16 [8, 1024, 1536], P('dp', 'seq')
- grad_signal: bfloat16 [8, 1024, 1536], P('dp', 'seq')
The draws below stay inside these ranges and needn't reach their ends.
All inputs are finite; a program needn't handle non-finite values.
Results may differ from the reference program's by a relative error of at most 0.0034.
Values may be sent and summed in bfloat16 or wider, within the bound.
No kernel may reach another device: no remote copies, remote signals or barrier semaphores. Data moves between devices by JAX's collectives and lax.ppermute only.
A program may use at most 64 MiB of HBM per device.

```python
import jax
import jax.numpy as jnp
from jax import lax

C = 1536
H = 768
DILATION_STEP = 32
WINDOWS = 8
WINDOW_BIN_COUNT = 1024


def shard_levels(stream_key, extent, pieces, least, top_value):
    loudness, own = 1.0, jax.random.fold_in(stream_key, 6)
    for dim, parts in pieces:
        draws = jnp.exp(jax.random.uniform(jax.random.fold_in(own, dim), (parts,), jnp.float32, least / len(pieces), top_value / len(pieces)))
        loudness = loudness * jnp.repeat(draws, extent[dim] // parts).reshape([-1 if axis == dim else 1 for axis in range(len(extent))])
    return loudness


def centred(own_key, extent, scale, limit, cuts=(), kind=jnp.bfloat16):
    gain = shard_levels(own_key, extent, cuts, -0.22, 0.18) if cuts else 1.0
    array = jax.random.normal(own_key, extent, jnp.float32) * scale * gain
    return jnp.minimum(jnp.maximum(array, -limit), limit).astype(kind)


def setup_inputs(seed: int = 0) -> dict:
    arg_keys = jax.random.split(jax.random.key(seed), 5)
    signal = centred(arg_keys[0], (WINDOWS, WINDOW_BIN_COUNT, C), 1.0, 6.0, ((0, 4), (1, 8)))
    dilated_tap_weight = centred(arg_keys[1], (3, C, H), (3 * C) ** -0.5, 0.09375, ((1, 4),))
    out_weight = centred(arg_keys[2], (H, C), H ** -0.5, 0.21875, ((1, 4),))
    cotangent = centred(arg_keys[3], (WINDOWS, WINDOW_BIN_COUNT, C), 1.0, 6.0, ((0, 4), (1, 8)))
    return {"signal": signal, "dilated_tap_weight": dilated_tap_weight, "out_weight": out_weight, "cotangent": cotangent}


def gelu_pull(point, grad):
    _, pull = jax.vjp(jax.nn.gelu, point)
    return pull(grad)[0]

def reference(signal, dilated_tap_weight, out_weight, cotangent):

    def one_window(inputs):
        window, grad_out = inputs
        gelu_output = jax.nn.gelu(window.astype(jnp.float32)).astype(jnp.bfloat16)
        padded_signal = jnp.pad(gelu_output, ((DILATION_STEP, DILATION_STEP), (0, 0)))
        preactivation = jnp.dot(padded_signal[0:WINDOW_BIN_COUNT], dilated_tap_weight[0], preferred_element_type=jnp.float32)
        preactivation = preactivation + jnp.dot(padded_signal[DILATION_STEP:DILATION_STEP + WINDOW_BIN_COUNT], dilated_tap_weight[1], preferred_element_type=jnp.float32)
        preactivation = preactivation + jnp.dot(padded_signal[2 * DILATION_STEP:2 * DILATION_STEP + WINDOW_BIN_COUNT], dilated_tap_weight[2], preferred_element_type=jnp.float32)
        active = jax.nn.gelu(preactivation).astype(jnp.bfloat16)
        output = (window.astype(jnp.float32) + jnp.dot(active, out_weight, preferred_element_type=jnp.float32)).astype(jnp.bfloat16)
        grad_active = jnp.dot(grad_out, out_weight.T, preferred_element_type=jnp.float32)
        gradient_preactivation = gelu_pull(preactivation, grad_active).astype(jnp.bfloat16)
        gradient_padded_input = jnp.pad(gradient_preactivation, ((DILATION_STEP, DILATION_STEP), (0, 0)))
        gradient_activation = jnp.dot(gradient_padded_input[2 * DILATION_STEP:2 * DILATION_STEP + WINDOW_BIN_COUNT], dilated_tap_weight[0].T, preferred_element_type=jnp.float32)
        gradient_activation = gradient_activation + jnp.dot(gradient_padded_input[DILATION_STEP:DILATION_STEP + WINDOW_BIN_COUNT], dilated_tap_weight[1].T, preferred_element_type=jnp.float32)
        gradient_activation = gradient_activation + jnp.dot(gradient_padded_input[0:WINDOW_BIN_COUNT], dilated_tap_weight[2].T, preferred_element_type=jnp.float32)
        grad_in = (grad_out.astype(jnp.float32) + gelu_pull(window.astype(jnp.float32), gradient_activation)).astype(jnp.bfloat16)
        return (output, grad_in)
    output, grad_in = lax.map(one_window, (signal, cotangent))
    return (output, grad_in)
```

```python
import functools
import jax
import jax.numpy as jnp
from jax import lax
from jax.experimental import pallas as pl
from jax.experimental.pallas import tpu as pltpu
from jax.sharding import PartitionSpec as P

DILATION_STEP = 32
PLANE = 8
F32 = jnp.float32
BF16 = jnp.bfloat16
ROOT = 0.7978845608028654
CUBIC = 0.044715


def gelu(v):
    return 0.5 * v * (1.0 + jnp.tanh(ROOT * (v + CUBIC * (v * v * v))))


def gelu_slope(v):
    square = v * v
    t = jnp.tanh(ROOT * v * (1.0 + CUBIC * square))
    return 0.5 * (1.0 + t) + (0.5 * ROOT) * v * (1.0 - t * t) * (1.0 + 3.0 * CUBIC * square)


def flip(index, bit):
    return index + bit - 2 * bit * ((index // bit) % 2)


def plane_pairs(count, bit_even, bit_odd):
    return [(i, i ^ (bit_odd if i % 2 else bit_even)) for i in range(count)]


def halo(block, width):
    count = lax.axis_size("seq")
    forward = [(i, i + 1) for i in range(count - 1)]
    backward = [(target, source) for source, target in forward]
    low = lax.ppermute(block[:, -width:], "seq", forward)
    high = lax.ppermute(block[:, :width], "seq", backward)
    return low, high


def stack_rows(ref, low, high, shift, columns):
    rows = ref.shape[1]
    parts = []
    for w in range(ref.shape[0]):
        if shift < 0:
            parts += [low[w, :, columns], ref[w, : rows + shift, columns]]
        elif shift > 0:
            parts += [ref[w, shift:, columns], high[w, :, columns]]
        else:
            parts += [ref[w, :, columns]]
    return jnp.concatenate(parts, axis=0)


def slot_dots(slot, taps, outs, act, low, high, cot):
    width = outs.shape[1]
    z = lax.axis_index("dp")
    for bit in (1, 2):
        if slot & bit:
            z = flip(z, bit)
    columns = pl.ds(pl.multiple_of(z * width, 128), width)
    inner = None
    for k in range(3):
        lhs = stack_rows(act, low, high, (k - 1) * DILATION_STEP, columns)
        term = jnp.dot(lhs, taps[k], preferred_element_type=F32)
        inner = term if inner is None else inner + term
    lhs = stack_rows(cot, None, None, 0, columns)
    grad = lax.dot_general(lhs, outs[...], (((1,), (1,)), ((), ())), preferred_element_type=F32)
    return inner, grad


def own_kernel(act, low, high, cot, taps, outs, inner, grad):
    inner[...], grad[...] = slot_dots(0, taps, outs, act, low, high, cot)


def slot_kernel(slot, act, low, high, cot, own, own_far, other, other_far, inner_in, grad_in, inner, grad, taps, outs, sems):
    s = lax.axis_index("seq") % PLANE
    rows = own.shape[2]
    width = outs.shape[1]
    first = 2 + 2 * (s % 2)
    second = 6 - first

    def moved(index, step):
        return index + step - 2 * step * ((index // step) % 2)

    mate = flip(s, 1)
    order = (
        (own, s, moved(s, first)),
        (own_far, moved(s, second), flip(flip(s, 2), 4)),
        (other, mate, moved(mate, second)),
        (other_far, moved(mate, first), flip(flip(mate, 2), 4)),
    )
    copies = []
    for buffer, *places in order:
        for i, q in enumerate(places):
            copies.append((buffer.at[i, 0:3], taps.at[:, pl.ds(pl.multiple_of(q * rows, 16), rows), :]))
            at = pl.multiple_of(q * 2 * rows, 16)
            copies.append((buffer.at[i, 3, :, 0:width], outs.at[pl.ds(at, rows), :]))
            copies.append((buffer.at[i, 3, :, width : 2 * width], outs.at[pl.ds(at + rows, rows), :]))
    copies = [pltpu.make_async_copy(a, b, sems.at[n]) for n, (a, b) in enumerate(copies)]
    for copy in copies:
        copy.start()
    for copy in copies:
        copy.wait()
    more_inner, more_grad = slot_dots(slot, taps, outs, act, low, high, cot)
    inner[...] = inner_in[...] + more_inner
    grad[...] = grad_in[...] + more_grad


def middle_kernel(inner, grad, active, grad_inner):
    v = inner[...]
    square = v * v
    t = jnp.tanh(ROOT * v * (1.0 + CUBIC * square))
    active[...] = (0.5 * v * (1.0 + t)).astype(BF16)
    slope = 0.5 * (1.0 + t) + (0.5 * ROOT) * v * (1.0 - t * t) * (1.0 + 3.0 * CUBIC * square)
    grad_inner[...] = (grad[...] * slope).astype(BF16).reshape(grad_inner.shape)


def slot_columns(slot, width):
    z = lax.axis_index("dp")
    for bit in (1, 2):
        if slot & bit:
            z = flip(z, bit)
    return pl.ds(pl.multiple_of(z * width, 128), width)


def result_kernel(slots, *refs):
    signal, active, grad_inner = refs[:3]
    taps = refs[3 : 3 + slots]
    outs = refs[3 + slots : 3 + 2 * slots]
    result, partial = refs[3 + 2 * slots :]
    width = outs[0].shape[1]
    windows, rows = signal.shape[:2]
    lhs = active[...]
    gi = grad_inner[...].reshape(windows * rows, -1)
    for slot in range(slots):
        columns = slot_columns(slot, width)
        more = jnp.dot(lhs, outs[slot][...], preferred_element_type=F32).reshape(windows, rows, width)
        result[:, :, columns] = (signal[:, :, columns].astype(F32) + more).astype(BF16)
        partial[:, :, columns] = lax.dot_general(
            gi, taps[slot][1], (((1,), (1,)), ((), ())), preferred_element_type=F32
        ).reshape(windows, rows, width)


def final_kernel(slots, *refs):
    cot, slope, partial, grad_inner, low, high = refs[:6]
    taps = refs[6 : 6 + slots]
    out = refs[6 + slots]
    windows, rows = cot.shape[:2]
    everything = slice(None)
    later = stack_rows(grad_inner, low, high, DILATION_STEP, everything)
    earlier = stack_rows(grad_inner, low, high, -DILATION_STEP, everything)
    width = taps[0].shape[1]
    dims = (((1,), (1,)), ((), ()))
    for slot in range(slots):
        columns = slot_columns(slot, width)
        more = lax.dot_general(later, taps[slot][0], dims, preferred_element_type=F32)
        more = more + lax.dot_general(earlier, taps[slot][2], dims, preferred_element_type=F32)
        total = partial[:, :, columns] + more.reshape(windows, rows, width)
        out[:, :, columns] = (cot[:, :, columns].astype(F32) + total * slope[:, :, columns]).astype(BF16)


def params(mib):
    return pltpu.CompilerParams(vmem_limit_bytes=mib << 20)


def per_device(slots, signal, tap, out, cot):
    windows, rows, channels = signal.shape
    hidden = tap.shape[2]
    width = tap.shape[1]
    total = windows * rows
    plane = lax.axis_index("seq") % PLANE
    piece = width // PLANE
    mine = lax.dynamic_slice_in_dim(tap, plane * piece, piece, axis=1)
    mine_out = lax.dynamic_slice_in_dim(out, plane * 2 * piece, 2 * piece, axis=0)
    mine = jnp.concatenate([mine, jnp.concatenate([mine_out[:piece], mine_out[piece:]], axis=1)[None]], axis=0)
    count = lax.axis_size("seq")
    gathered = []
    for slot in range(1, slots):
        got = lax.ppermute(mine, "dp", [(i, i ^ slot) for i in range(slots)])
        near = lax.ppermute(got, "seq", plane_pairs(count, 2, 4))
        own = jnp.stack([got, near])
        own_far = lax.ppermute(own, "seq", plane_pairs(count, 4, 2))
        other = lax.ppermute(own, "seq", plane_pairs(count, 1, 1))
        other_far = lax.ppermute(own_far, "seq", plane_pairs(count, 1, 1))
        gathered.append((own, own_far, other, other_far))

    wide = signal.astype(F32)
    act = gelu(wide).astype(BF16)
    slope = gelu_slope(wide)
    low, high = halo(act, DILATION_STEP)

    sums = [jax.ShapeDtypeStruct((total, hidden), F32)] * 2
    vmem = pl.BlockSpec(memory_space=pltpu.VMEM)
    hbm = pl.BlockSpec(memory_space=pl.ANY)
    inner, grad = pl.pallas_call(
        own_kernel, out_shape=sums, in_specs=[vmem] * 6, out_specs=[vmem] * 2, compiler_params=params(24)
    )(act, low, high, cot, tap, out)
    taps, outs = [tap], [out]
    for slot in range(1, slots):
        inner, grad, more_tap, more_out = pl.pallas_call(
            functools.partial(slot_kernel, slot),
            out_shape=sums + [jax.ShapeDtypeStruct(tap.shape, BF16), jax.ShapeDtypeStruct(out.shape, BF16)],
            in_specs=[vmem] * 4 + [hbm] * 4 + [vmem] * 2,
            out_specs=[vmem] * 4,
            scratch_shapes=[pltpu.SemaphoreType.DMA((24,))],
            input_output_aliases={8: 0, 9: 1},
            compiler_params=params(24),
        )(act, low, high, cot, *gathered[slot - 1], inner, grad)
        taps.append(more_tap)
        outs.append(more_out)
    active, grad_inner = pl.pallas_call(
        middle_kernel,
        out_shape=[jax.ShapeDtypeStruct((total, hidden), BF16), jax.ShapeDtypeStruct((windows, rows, hidden), BF16)],
        in_specs=[vmem] * 2,
        out_specs=[vmem] * 2,
        compiler_params=params(16),
    )(inner, grad)
    low, high = halo(grad_inner, DILATION_STEP)
    result, partial = pl.pallas_call(
        functools.partial(result_kernel, slots),
        out_shape=[jax.ShapeDtypeStruct(signal.shape, BF16), jax.ShapeDtypeStruct(signal.shape, F32)],
        in_specs=[vmem] * (3 + 2 * slots),
        out_specs=[vmem] * 2,
        compiler_params=params(32),
    )(signal, active, grad_inner, *taps, *outs)
    grad_signal = pl.pallas_call(
        functools.partial(final_kernel, slots),
        out_shape=jax.ShapeDtypeStruct(signal.shape, BF16),
        in_specs=[vmem] * (6 + slots),
        out_specs=vmem,
        compiler_params=params(32),
    )(cot, slope, partial, grad_inner, low, high, *taps)
    return result, grad_signal


def extended(block, width):
    low, high = halo(block, width)
    return jnp.concatenate([low, block, high], axis=1)


def per_device_general(signal, tap, out, cot):
    tap = lax.all_gather(tap, "dp", axis=1, tiled=True)
    out = lax.all_gather(out, "dp", axis=1, tiled=True)
    rows = signal.shape[1]
    wide = signal.astype(F32)
    act = extended(gelu(wide).astype(BF16), DILATION_STEP)

    def contract(rule, a, b):
        return jnp.einsum(rule, a, b, preferred_element_type=F32)

    def window(block, k):
        return block[:, k * DILATION_STEP : k * DILATION_STEP + rows]

    inner = sum(contract("wtc,ch->wth", window(act, k), tap[k]) for k in range(3))
    active = gelu(inner).astype(BF16)
    result = wide + contract("wth,hc->wtc", active, out)
    grad_inner = (contract("wtc,hc->wth", cot, out) * gelu_slope(inner)).astype(BF16)
    grad_inner = extended(grad_inner, DILATION_STEP)
    grad_act = sum(contract("wth,ch->wtc", window(grad_inner, 2 - k), tap[k]) for k in range(3))
    grad_signal = cot.astype(F32) + grad_act * gelu_slope(wide)
    return result.astype(BF16), grad_signal.astype(BF16)


def solution(mesh):
    dp, seq = mesh.shape["dp"], mesh.shape["seq"]

    def run(signal, tap, out, cot):
        width = tap.shape[1] // dp
        hidden = tap.shape[2]
        sliced = dp in (2, 4) and seq % PLANE == 0 and width % 128 == 0 and 2 * width == hidden
        body = functools.partial(per_device, dp) if sliced else per_device_general
        return jax.shard_map(
            body,
            mesh=mesh,
            in_specs=(P("dp", "seq", None), P(None, "dp", None), P(None, "dp"), P("dp", "seq", None)),
            out_specs=(P("dp", "seq", None), P("dp", "seq", None)),
            check_vma=False,
        )(signal, tap, out, cot)

    return run
```

```python
import functools
import jax
import jax.numpy as jnp
from jax import lax
from jax.experimental import pallas as pl
from jax.experimental.pallas import tpu as pltpu
from jax.sharding import PartitionSpec as P

DILATION_STEP = 32
PLANE = 8
F32 = jnp.float32
BF16 = jnp.bfloat16
ROOT = 0.7978845608028654
CUBIC = 0.044715


def gelu(v):
    return 0.5 * v * (1.0 + jnp.tanh(ROOT * (v + CUBIC * (v * v * v))))


def gelu_slope(v):
    square = v * v
    t = jnp.tanh(ROOT * v * (1.0 + CUBIC * square))
    return 0.5 * (1.0 + t) + (0.5 * ROOT) * v * (1.0 - t * t) * (1.0 + 3.0 * CUBIC * square)


def flip(index, bit):
    return index + bit - 2 * bit * ((index // bit) % 2)


def halo(block, width):
    count = lax.axis_size("seq")
    forward = [(i, i + 1) for i in range(count - 1)]
    backward = [(target, source) for source, target in forward]
    low = lax.ppermute(block[:, -width:], "seq", forward)
    high = lax.ppermute(block[:, :width], "seq", backward)
    return low, high


def plane_pairs(count, bit_even, bit_odd):
    return [(i, i ^ (bit_odd if i % 2 else bit_even)) for i in range(count)]


def slot_columns(slot, width):
    z = lax.axis_index("dp")
    upper = z // 2
    shard = (z, flip(z, 1), 2 - upper, 3 - 3 * upper)[slot]
    return pl.ds(pl.multiple_of(shard * width, 128), width)


def held(name):
    s = lax.axis_index("seq") % PLANE

    def moved(index, step):
        return index + step - 2 * step * ((index // step) % 2)

    first = 2 + 2 * (s % 2)
    second = 6 - first
    mate = flip(s, 1)
    return {
        "near": (s, moved(s, first)),
        "far": (moved(s, second), flip(flip(s, 2), 4)),
        "mate_near": (mate, moved(mate, second)),
        "mate_far": (moved(mate, first), flip(flip(mate, 2), 4)),
    }[name]


def slice_kernel(tap, out, piece, stage, sem):
    s = lax.axis_index("seq") % PLANE
    matrix, half = s // 2, s % 2
    size = piece.shape[0]
    part = pl.ds(pl.multiple_of(half * size, 128), size)

    @pl.when(matrix < 3)
    def _():
        copy = pltpu.make_async_copy(tap.at[matrix, :, part], piece, sem)
        copy.start()
        copy.wait()

    @pl.when(matrix == 3)
    def _():
        copy = pltpu.make_async_copy(out.at[part, :], stage, sem)
        copy.start()
        copy.wait()
        piece[...] = stage[...].T


def left_kernel(signal, cot, low, high, left, slope):
    reach = 2 * DILATION_STEP
    windows, rows, _ = signal.shape
    for w in range(windows):
        wide = signal[w].astype(F32)
        square = wide * wide
        t = jnp.tanh(ROOT * wide * (1.0 + CUBIC * square))
        left[0, w, reach : reach + rows] = (0.5 * wide * (1.0 + t)).astype(BF16)
        slope[w] = 0.5 * (1.0 + t) + (0.5 * ROOT) * wide * (1.0 - t * t) * (1.0 + 3.0 * CUBIC * square)
        left[0, w, 0:reach] = gelu(low[w, 0:reach].astype(F32)).astype(BF16)
        left[0, w, reach + rows :] = gelu(high[w, DILATION_STEP:].astype(F32)).astype(BF16)
        left[1, w, 0:DILATION_STEP] = low[w, reach:]
        left[1, w, DILATION_STEP : DILATION_STEP + rows] = cot[w]
        left[1, w, DILATION_STEP + rows : reach + rows] = high[w, 0:DILATION_STEP]
        left[1, w, reach + rows :] = jnp.zeros_like(left[1, w, reach + rows :])


def rows_of(left, which, offset, rows, columns):
    return jnp.concatenate([left[which, w, pl.ds(offset, rows), columns] for w in range(left.shape[1])], axis=0)


LAST = (((1,), (1,)), ((), ()))


def own_kernel(left, tap, out, sums):
    rows = left.shape[2] - 2 * DILATION_STEP
    columns = slot_columns(0, tap.shape[1])
    inner = None
    for k in range(3):
        term = jnp.dot(rows_of(left, 0, k * DILATION_STEP, rows, columns), tap[k], preferred_element_type=F32)
        inner = term if inner is None else inner + term
    sums[0] = inner
    sums[1] = lax.dot_general(rows_of(left, 1, 0, rows, columns), out[...], LAST, preferred_element_type=F32)


def slot_kernel(slot, names, fresh, *refs):
    count = len(names)
    left, sums_in = refs[0], refs[1]
    buffers = refs[2 : 2 + count]
    sums, whole, sems = refs[-3:]
    rows = left.shape[2] - 2 * DILATION_STEP
    size = buffers[0].shape[1]
    columns = slot_columns(slot, size)
    pieces = [(b, i, q) for b, name in zip(buffers, names) for i, q in enumerate(held(name))]
    copies = []
    for n, (buffer, i, q) in enumerate(pieces):
        half = pl.ds(pl.multiple_of((q % 2) * size, 128), size)
        copies.append(pltpu.make_async_copy(buffer.at[i], whole.at[q // 2, :, half], sems.at[n]))
        copies[-1].start()
    for buffer, name in zip(buffers, names):
        terms = []
        for i, q in enumerate(held(name)):
            matrix = q // 2
            offset = pl.multiple_of((matrix % 3) * DILATION_STEP, DILATION_STEP)
            lhs = rows_of(left, matrix // 3, offset, rows, columns)
            terms.append((matrix // 3, jnp.dot(lhs, buffer[i], preferred_element_type=F32)))
        half = pl.ds(pl.multiple_of((held(name)[0] % 2) * size, 128), size)
        for which in range(2):
            total = sums_in[which, :, half]
            for place, term in terms:
                total = total + jnp.where(place == which, term, 0.0)
            sums[which, :, half] = total
    for copy in copies:
        copy.wait()


def middle_kernel(sums, right):
    windows, rows = right.shape[1:3]
    v = sums[0]
    square = v * v
    t = jnp.tanh(ROOT * v * (1.0 + CUBIC * square))
    slope = 0.5 * (1.0 + t) + (0.5 * ROOT) * v * (1.0 - t * t) * (1.0 + 3.0 * CUBIC * square)
    right[0] = (sums[1] * slope).astype(BF16).reshape(right.shape[1:])
    active = (0.5 * v * (1.0 + t)).astype(BF16).reshape(right.shape[1:])
    right[1, :, 2 * DILATION_STEP :] = active[:, DILATION_STEP : rows - DILATION_STEP]


def back_kernel(signal, cot, slope, right, tap, out, *refs):
    wholes, (result, grad) = refs[:3], refs[3:]
    windows, rows, _ = signal.shape
    width = tap.shape[1]
    step = DILATION_STEP
    everything = slice(None)
    shifted = [rows_of(right, 0, (2 - k) * step, rows, everything) for k in range(3)]
    active = rows_of(right, 1, 2 * step, rows, everything)
    for slot in range(4):
        columns = slot_columns(slot, width)
        matrices = tap if slot == 0 else wholes[slot - 1]
        total = None
        for k in range(3):
            term = lax.dot_general(shifted[k], matrices[k], LAST, preferred_element_type=F32)
            total = term if total is None else total + term
        if slot == 0:
            more = jnp.dot(active, out[...], preferred_element_type=F32)
        else:
            more = lax.dot_general(active, matrices[3], LAST, preferred_element_type=F32)
        for w in range(windows):
            at = slice(w * rows, (w + 1) * rows)
            grad[w, :, columns] = (cot[w, :, columns].astype(F32) + total[at] * slope[w, :, columns]).astype(BF16)
            result[w, :, columns] = (signal[w, :, columns].astype(F32) + more[at]).astype(BF16)


def cost(microseconds):
    return pl.CostEstimate(flops=int(microseconds * 9e8), bytes_accessed=int(microseconds * 3e6), transcendentals=0)


def params(mib):
    return pltpu.CompilerParams(vmem_limit_bytes=mib << 20)


def tie(*values):
    return lax.optimization_barrier(values)


def per_device(signal, tap, out, cot):
    windows, rows, channels = signal.shape
    hidden = tap.shape[2]
    width = tap.shape[1]
    wide_rows = rows + 2 * DILATION_STEP
    vmem = pl.BlockSpec(memory_space=pltpu.VMEM)
    hbm = pl.BlockSpec(memory_space=pl.ANY)
    count = lax.axis_size("seq")
    z = lax.axis_index("dp")
    middle = (z == 1) | (z == 2)

    mine = pl.pallas_call(
        slice_kernel,
        out_shape=jax.ShapeDtypeStruct((width, width), BF16),
        in_specs=[hbm] * 2,
        out_specs=vmem,
        scratch_shapes=[pltpu.VMEM((width, width), BF16), pltpu.SemaphoreType.DMA],
        compiler_params=params(60),
    )(tap, out)

    def across(block, even, odd):
        return lax.ppermute(block, "seq", plane_pairs(count, even, odd))

    outward = [(1, 0), (2, 3)]
    inward = [(1, 2), (2, 1)]
    sums_shape = jax.ShapeDtypeStruct((2, windows * wide_rows, hidden), F32)
    whole_shape = jax.ShapeDtypeStruct((4, width, hidden), BF16)

    def add_slot(slot, names, buffers, left, sums, whole=None):
        fresh = whole is None
        given = [left, sums, *buffers] + ([] if fresh else [whole])
        aliases = {1: 0}
        if not fresh:
            aliases[len(given) - 1] = 1
        return pl.pallas_call(
            functools.partial(slot_kernel, slot, names, fresh),
            out_shape=[sums_shape, whole_shape],
            in_specs=[vmem] * len(given),
            out_specs=[vmem] * 2,
            scratch_shapes=[pltpu.SemaphoreType.DMA((2 * len(names),))],
            input_output_aliases=aliases,
            compiler_params=params(16),
            cost_estimate=cost(0.5 * len(names)),
        )(*given)

    p1 = lax.ppermute(mine, "dp", [(0, 1), (1, 0), (2, 3), (3, 2)])
    reach = 2 * DILATION_STEP
    low, high = (
        jnp.concatenate([signal[:, -reach:], cot[:, -DILATION_STEP:]], axis=1),
        jnp.concatenate([cot[:, :DILATION_STEP], signal[:, :reach]], axis=1),
    )
    low, high, mine = tie(low, high, mine)
    p2 = lax.ppermute(mine, "dp", inward)
    low = lax.ppermute(low, "seq", [(i, i + 1) for i in range(count - 1)])
    high = lax.ppermute(high, "seq", [(i + 1, i) for i in range(count - 1)])

    near1 = across(p1, 2, 4)
    p4 = lax.ppermute(p1, "dp", inward)
    p3 = lax.ppermute(p2, "dp", outward)
    left, slope = pl.pallas_call(
        left_kernel,
        out_shape=[
            jax.ShapeDtypeStruct((2, windows, rows + 2 * reach, channels), BF16),
            jax.ShapeDtypeStruct(signal.shape, F32),
        ],
        in_specs=[vmem] * 4,
        out_specs=[vmem] * 2,
        compiler_params=params(16),
        cost_estimate=cost(2.5),
    )(signal, cot, low, high)
    sums = pl.pallas_call(
        own_kernel,
        out_shape=sums_shape,
        in_specs=[vmem] * 3,
        out_specs=vmem,
        compiler_params=params(16),
        cost_estimate=cost(1.5),
    )(left, tap, out)
    own1 = jnp.stack([p1, near1])
    far1 = across(own1, 4, 2)
    mate1 = across(own1, 1, 1)
    got2 = jnp.where(middle, p2, p3)
    near2 = across(got2, 2, 4)
    p5 = lax.ppermute(p4, "dp", outward)
    near_names, far_names = ("near", "mate_near"), ("far", "mate_far")
    own2 = jnp.stack([got2, near2])
    own2, sums = tie(own2, sums)
    far2 = across(own2, 4, 2)
    mate2 = across(own2, 1, 1)
    far_mate1 = across(far1, 1, 1)
    sums, whole1 = add_slot(1, near_names, (own1, mate1), left, sums)
    got3 = jnp.where(middle, p4, p5)
    got3, sums = tie(got3, sums)
    near3 = across(got3, 2, 4)
    own3 = jnp.stack([got3, near3])
    sums, whole1 = add_slot(1, far_names, (far1, far_mate1), left, sums, whole1)
    own3, sums = tie(own3, sums)
    far3 = across(own3, 4, 2)
    mate3 = across(own3, 1, 1)
    far_mate2 = across(far2, 1, 1)
    sums, whole2 = add_slot(2, near_names, (own2, mate2), left, sums)
    sums, whole2 = add_slot(2, far_names, (far2, far_mate2), left, sums, whole2)
    sums, whole3 = add_slot(3, near_names, (own3, mate3), left, sums)
    far3, sums = tie(far3, sums)
    far_mate3 = across(far3, 1, 1)
    sums, whole3 = add_slot(3, far_names, (far3, far_mate3), left, sums, whole3)

    right = pl.pallas_call(
        middle_kernel,
        out_shape=jax.ShapeDtypeStruct((2, windows, wide_rows, hidden), BF16),
        in_specs=[vmem],
        out_specs=vmem,
        compiler_params=params(16),
        cost_estimate=cost(0.8),
    )(sums)
    result, grad_signal = pl.pallas_call(
        back_kernel,
        out_shape=[jax.ShapeDtypeStruct(signal.shape, BF16)] * 2,
        in_specs=[vmem] * 9,
        out_specs=[vmem] * 2,
        compiler_params=params(24),
        cost_estimate=cost(4.5),
    )(signal, cot, slope, right, tap, out, whole1, whole2, whole3)
    return result, grad_signal


def extended(block, width):
    low, high = halo(block, width)
    return jnp.concatenate([low, block, high], axis=1)


def per_device_general(signal, tap, out, cot):
    tap = lax.all_gather(tap, "dp", axis=1, tiled=True)
    out = lax.all_gather(out, "dp", axis=1, tiled=True)
    rows = signal.shape[1]
    wide = signal.astype(F32)
    act = extended(gelu(wide).astype(BF16), DILATION_STEP)

    def contract(rule, a, b):
        return jnp.einsum(rule, a, b, preferred_element_type=F32)

    def window(block, k):
        return block[:, k * DILATION_STEP : k * DILATION_STEP + rows]

    inner = sum(contract("wtc,ch->wth", window(act, k), tap[k]) for k in range(3))
    active = gelu(inner).astype(BF16)
    result = wide + contract("wth,hc->wtc", active, out)
    grad_inner = (contract("wtc,hc->wth", cot, out) * gelu_slope(inner)).astype(BF16)
    grad_inner = extended(grad_inner, DILATION_STEP)
    grad_act = sum(contract("wth,ch->wtc", window(grad_inner, 2 - k), tap[k]) for k in range(3))
    grad_signal = cot.astype(F32) + grad_act * gelu_slope(wide)
    return result.astype(BF16), grad_signal.astype(BF16)


def solution(mesh):
    dp, seq = mesh.shape["dp"], mesh.shape["seq"]

    def run(signal, tap, out, cot):
        width = tap.shape[1] // dp
        hidden = tap.shape[2]
        sliced = dp == 4 and seq % PLANE == 0 and width % 128 == 0 and 2 * width == hidden
        body = per_device if sliced else per_device_general
        return jax.shard_map(
            body,
            mesh=mesh,
            in_specs=(P("dp", "seq", None), P(None, "dp", None), P(None, "dp"), P("dp", "seq", None)),
            out_specs=(P("dp", "seq", None), P("dp", "seq", None)),
            check_vma=False,
        )(signal, tap, out, cot)

    return run
```

```python
import functools
import jax
import jax.numpy as jnp
from jax import lax
from jax.experimental import pallas as pl
from jax.experimental.pallas import tpu as pltpu
from jax.sharding import PartitionSpec as P

DILATION_STEP = 32
PLANE = 8
F32 = jnp.float32
BF16 = jnp.bfloat16
ROOT = 0.7978845608028654
CUBIC = 0.044715


def gelu(v):
    return 0.5 * v * (1.0 + jnp.tanh(ROOT * (v + CUBIC * (v * v * v))))


def gelu_slope(v):
    square = v * v
    t = jnp.tanh(ROOT * v * (1.0 + CUBIC * square))
    return 0.5 * (1.0 + t) + (0.5 * ROOT) * v * (1.0 - t * t) * (1.0 + 3.0 * CUBIC * square)


def flip(index, bit):
    return index + bit - 2 * bit * ((index // bit) % 2)


def halo(block, width):
    count = lax.axis_size("seq")
    forward = [(i, i + 1) for i in range(count - 1)]
    backward = [(target, source) for source, target in forward]
    low = lax.ppermute(block[:, -width:], "seq", forward)
    high = lax.ppermute(block[:, :width], "seq", backward)
    return low, high


def plane_pairs(count, bit_even, bit_odd):
    return [(i, i ^ (bit_odd if i % 2 else bit_even)) for i in range(count)]


def slot_columns(slot, width):
    z = lax.axis_index("dp")
    for bit in (1, 2):
        if slot & bit:
            z = flip(z, bit)
    return pl.ds(pl.multiple_of(z * width, 128), width)


def held(name):
    s = lax.axis_index("seq") % PLANE

    def moved(index, step):
        return index + step - 2 * step * ((index // step) % 2)

    first = 2 + 2 * (s % 2)
    second = 6 - first
    mate = flip(s, 1)
    return {
        "near": (s, moved(s, first)),
        "far": (moved(s, second), flip(flip(s, 2), 4)),
        "mate_near": (mate, moved(mate, second)),
        "mate_far": (moved(mate, first), flip(flip(mate, 2), 4)),
        "first": (s % 2,),
        "last": (2 + s % 2, 4 + s % 2, 6 + s % 2),
        "mate_first": (mate % 2,),
        "mate_last": (2 + mate % 2, 4 + mate % 2, 6 + mate % 2),
    }[name]


def prepare_kernel(signal, cot, tap, out, piece, first, to_next, to_previous, stage, sem, sems):
    s = lax.axis_index("seq") % PLANE
    matrix, half = s // 2, s % 2
    size = piece.shape[0]
    rows = signal.shape[1]
    step = DILATION_STEP
    part = pl.ds(pl.multiple_of(half * size, 128), size)
    copies = [
        (tap.at[0:1, :, part], first),
        (signal.at[:, rows - 2 * step :], to_next.at[:, 0 : 2 * step]),
        (cot.at[:, rows - step :], to_next.at[:, 2 * step :]),
        (cot.at[:, 0:step], to_previous.at[:, 0:step]),
        (signal.at[:, 0 : 2 * step], to_previous.at[:, step:]),
    ]
    copies = [pltpu.make_async_copy(a, b, sems.at[n]) for n, (a, b) in enumerate(copies)]

    @pl.when(matrix < 3)
    def _():
        copy = pltpu.make_async_copy(tap.at[matrix, :, part], piece, sem)
        copy.start()
        for other in copies:
            other.start()
        copy.wait()

    @pl.when(matrix == 3)
    def _():
        copy = pltpu.make_async_copy(out.at[part, :], stage, sem)
        copy.start()
        for other in copies:
            other.start()
        copy.wait()
        piece[...] = stage[...].T

    for other in copies:
        other.wait()


def half_kernel(tap, out, last, stage, sems):
    half = lax.axis_index("seq") % 2
    size = last.shape[1]
    part = pl.ds(pl.multiple_of(half * size, 128), size)
    copies = [(out.at[part, :], stage), (tap.at[1:3, :, part], last.at[0:2])]
    copies = [pltpu.make_async_copy(a, b, sems.at[n]) for n, (a, b) in enumerate(copies)]
    for copy in copies:
        copy.start()
    copies[0].wait()
    last[2] = stage[...].T
    copies[1].wait()


def left_kernel(signal, cot, left, slope):
    reach = 2 * DILATION_STEP
    windows, rows, _ = signal.shape
    for w in range(windows):
        wide = signal[w].astype(F32)
        square = wide * wide
        t = jnp.tanh(ROOT * wide * (1.0 + CUBIC * square))
        left[0, w, reach : reach + rows] = (0.5 * wide * (1.0 + t)).astype(BF16)
        slope[w] = 0.5 * (1.0 + t) + (0.5 * ROOT) * wide * (1.0 - t * t) * (1.0 + 3.0 * CUBIC * square)
        left[1, w, DILATION_STEP : DILATION_STEP + rows] = cot[w]
        left[1, w, reach + rows :] = jnp.zeros_like(left[1, w, reach + rows :])


def pair_kernel(first, second, both, sems):
    copies = [pltpu.make_async_copy(a, both.at[n], sems.at[n]) for n, a in enumerate((first, second))]
    for copy in copies:
        copy.start()
    for copy in copies:
        copy.wait()


def edge_kernel(low, high, left_in, left, sems):
    reach = 2 * DILATION_STEP
    windows = low.shape[0]
    rows = left.shape[2] - 2 * reach
    copies = [
        (low.at[:, reach:], left.at[1, :, 0:DILATION_STEP]),
        (high.at[:, 0:DILATION_STEP], left.at[1, :, DILATION_STEP + rows : reach + rows]),
    ]
    copies = [pltpu.make_async_copy(a, b, sems.at[n]) for n, (a, b) in enumerate(copies)]
    for copy in copies:
        copy.start()
    for w in range(windows):
        left[0, w, 0:reach] = gelu(low[w, 0:reach].astype(F32)).astype(BF16)
        left[0, w, reach + rows :] = gelu(high[w, DILATION_STEP:].astype(F32)).astype(BF16)
    for copy in copies:
        copy.wait()


def rows_of(left, which, offset, rows, columns):
    return jnp.concatenate([left[which, w, pl.ds(offset, rows), columns] for w in range(left.shape[1])], axis=0)


LAST = (((1,), (1,)), ((), ()))


def own_kernel(left, tap, out, sums):
    rows = left.shape[2] - 2 * DILATION_STEP
    columns = slot_columns(0, tap.shape[1])
    inner = None
    for k in range(3):
        term = jnp.dot(rows_of(left, 0, k * DILATION_STEP, rows, columns), tap[k], preferred_element_type=F32)
        inner = term if inner is None else inner + term
    sums[0] = inner
    sums[1] = lax.dot_general(rows_of(left, 1, 0, rows, columns), out[...], LAST, preferred_element_type=F32)


def slot_kernel(slot, names, fresh, *refs):
    count = len(names)
    left, sums_in = refs[0], refs[1]
    buffers = refs[2 : 2 + count]
    sums, whole, sems = refs[-3:]
    rows = left.shape[2] - 2 * DILATION_STEP
    size = buffers[0].shape[1]
    columns = slot_columns(slot, size)
    pieces = [(b, i, q) for b, name in zip(buffers, names) for i, q in enumerate(held(name))]
    copies = []
    for n, (buffer, i, q) in enumerate(pieces):
        half = pl.ds(pl.multiple_of((q % 2) * size, 128), size)
        copies.append(pltpu.make_async_copy(buffer.at[i], whole.at[q // 2, :, half], sems.at[n]))
        copies[-1].start()
    for buffer, name in zip(buffers, names):
        terms = []
        for i, q in enumerate(held(name)):
            matrix = q // 2
            offset = pl.multiple_of((matrix % 3) * DILATION_STEP, DILATION_STEP)
            lhs = rows_of(left, matrix // 3, offset, rows, columns)
            terms.append((matrix // 3, jnp.dot(lhs, buffer[i], preferred_element_type=F32)))
        half = pl.ds(pl.multiple_of((held(name)[0] % 2) * size, 128), size)
        for which in range(2):
            total = sums_in[which, :, half]
            for place, term in terms:
                total = total + jnp.where(place == which, term, 0.0)
            sums[which, :, half] = total
    for copy in copies:
        copy.wait()


def middle_kernel(sums, right):
    windows, rows = right.shape[1:3]
    v = sums[0]
    square = v * v
    t = jnp.tanh(ROOT * v * (1.0 + CUBIC * square))
    slope = 0.5 * (1.0 + t) + (0.5 * ROOT) * v * (1.0 - t * t) * (1.0 + 3.0 * CUBIC * square)
    right[0] = (sums[1] * slope).astype(BF16).reshape(right.shape[1:])
    active = (0.5 * v * (1.0 + t)).astype(BF16).reshape(right.shape[1:])
    right[1, :, 2 * DILATION_STEP :] = active[:, DILATION_STEP : rows - DILATION_STEP]


def back_kernel(signal, cot, slope, right, tap, out, *refs):
    wholes, (result, grad) = refs[:3], refs[3:]
    windows, rows, _ = signal.shape
    width = tap.shape[1]
    step = DILATION_STEP
    everything = slice(None)
    shifted = [rows_of(right, 0, (2 - k) * step, rows, everything) for k in range(3)]
    active = rows_of(right, 1, 2 * step, rows, everything)
    for slot in range(4):
        columns = slot_columns(slot, width)
        matrices = tap if slot == 0 else wholes[slot - 1]
        total = None
        for k in range(3):
            term = lax.dot_general(shifted[k], matrices[k], LAST, preferred_element_type=F32)
            total = term if total is None else total + term
        if slot == 0:
            more = jnp.dot(active, out[...], preferred_element_type=F32)
        else:
            more = lax.dot_general(active, matrices[3], LAST, preferred_element_type=F32)
        for w in range(windows):
            at = slice(w * rows, (w + 1) * rows)
            grad[w, :, columns] = (cot[w, :, columns].astype(F32) + total[at] * slope[w, :, columns]).astype(BF16)
            result[w, :, columns] = (signal[w, :, columns].astype(F32) + more[at]).astype(BF16)


def cost(microseconds):
    return pl.CostEstimate(flops=1000, bytes_accessed=1000, transcendentals=0)


def params(mib):
    return pltpu.CompilerParams(vmem_limit_bytes=mib << 20)


def tie(*values):
    return lax.optimization_barrier(values)


def per_device(signal, tap, out, cot):
    windows, rows, channels = signal.shape
    hidden = tap.shape[2]
    width = tap.shape[1]
    wide_rows = rows + 2 * DILATION_STEP
    vmem = pl.BlockSpec(memory_space=pltpu.VMEM)
    hbm = pl.BlockSpec(memory_space=pl.ANY)
    count = lax.axis_size("seq")

    def stay(array):
        return pltpu.with_memory_space_constraint(array, pltpu.HBM)

    reach = 2 * DILATION_STEP
    edge = jax.ShapeDtypeStruct((windows, reach + DILATION_STEP, channels), BF16)
    mine, first, low, high = pl.pallas_call(
        prepare_kernel,
        out_shape=[
            jax.ShapeDtypeStruct((width, width), BF16),
            jax.ShapeDtypeStruct((1, width, width), BF16),
            edge,
            edge,
        ],
        in_specs=[hbm] * 4,
        out_specs=[vmem] * 4,
        scratch_shapes=[
            pltpu.VMEM((width, width), BF16),
            pltpu.SemaphoreType.DMA,
            pltpu.SemaphoreType.DMA((5,)),
        ],
        compiler_params=params(8),
    )(stay(signal), stay(cot), stay(tap), stay(out))

    def across(block, even, odd):
        return lax.ppermute(block, "seq", plane_pairs(count, even, odd))

    def over(block, bits):
        return lax.ppermute(block, "dp", [(i, i ^ bits) for i in range(4)])

    def pair(first, second):
        return pl.pallas_call(
            pair_kernel,
            out_shape=jax.ShapeDtypeStruct((2, width, width), BF16),
            in_specs=[hbm] * 2,
            out_specs=vmem,
            scratch_shapes=[pltpu.SemaphoreType.DMA((2,))],
            compiler_params=params(2),
            cost_estimate=cost(0.3),
        )(first, second)

    sums_shape = jax.ShapeDtypeStruct((2, windows * wide_rows, hidden), F32)
    whole_shape = jax.ShapeDtypeStruct((4, width, hidden), BF16)

    def add_slot(slot, names, buffers, left, sums, whole=None):
        fresh = whole is None
        given = [left, sums, *buffers] + ([] if fresh else [whole])
        aliases = {1: 0}
        if not fresh:
            aliases[len(given) - 1] = 1
        return pl.pallas_call(
            functools.partial(slot_kernel, slot, names, fresh),
            out_shape=[sums_shape, whole_shape],
            in_specs=[vmem] * len(given),
            out_specs=[vmem] * 2,
            scratch_shapes=[pltpu.SemaphoreType.DMA((sum(b.shape[0] for b in buffers),))],
            input_output_aliases=aliases,
            compiler_params=params(4),
            cost_estimate=cost(0.7 * len(names)),
        )(*given)

    p2 = over(mine, 2)
    first = over(first, 1)
    low = lax.ppermute(low, "seq", [(i, i + 1) for i in range(count - 1)])
    high = lax.ppermute(high, "seq", [(i + 1, i) for i in range(count - 1)])
    left_shape = jax.ShapeDtypeStruct((2, windows, rows + 2 * reach, channels), BF16)
    left, slope = pl.pallas_call(
        left_kernel,
        out_shape=[left_shape, jax.ShapeDtypeStruct(signal.shape, F32)],
        in_specs=[vmem] * 2,
        out_specs=[vmem] * 2,
        compiler_params=params(4),
        cost_estimate=cost(1.3),
    )(signal, cot)
    last = pl.pallas_call(
        half_kernel,
        out_shape=jax.ShapeDtypeStruct((3, width, width), BF16),
        in_specs=[hbm] * 2,
        out_specs=vmem,
        scratch_shapes=[pltpu.VMEM((width, width), BF16), pltpu.SemaphoreType.DMA((2,))],
        compiler_params=params(4),
        cost_estimate=cost(1.5),
    )(stay(tap), stay(out))
    p2, first, left, last = tie(p2, first, left, last)
    near2 = across(p2, 2, 4)
    p3 = over(p2, 1)
    left = pl.pallas_call(
        edge_kernel,
        out_shape=left_shape,
        in_specs=[vmem] * 3,
        out_specs=vmem,
        scratch_shapes=[pltpu.SemaphoreType.DMA((2,))],
        input_output_aliases={2: 0},
        compiler_params=params(4),
        cost_estimate=cost(0.5),
    )(low, high, left)
    sums = pl.pallas_call(
        own_kernel,
        out_shape=sums_shape,
        in_specs=[vmem] * 3,
        out_specs=vmem,
        compiler_params=params(4),
        cost_estimate=cost(1.4),
    )(left, tap, out)
    near_names, far_names = ("near", "mate_near"), ("far", "mate_far")
    mate_first = across(first, 1, 1)
    own2 = pair(p2, near2)
    own2, left = tie(own2, left)
    far2 = across(own2, 4, 2)
    mate2 = across(own2, 1, 1)
    p3, last = tie(p3, last)
    near3 = across(p3, 2, 4)
    last = over(last, 1)
    far_mate2 = across(far2, 1, 1)
    own3 = pair(p3, near3)
    own3, sums = tie(own3, sums)
    far3 = across(own3, 4, 2)
    mate3 = across(own3, 1, 1)
    sums, whole2 = add_slot(2, near_names, (own2, mate2), left, sums)
    sums, whole1 = add_slot(1, ("first", "mate_first"), (first, mate_first), left, sums)
    sums, whole3 = add_slot(3, near_names, (own3, mate3), left, sums)
    last, sums = tie(last, sums)
    mate_last = across(last, 1, 1)
    sums, whole2 = add_slot(2, far_names, (far2, far_mate2), left, sums, whole2)
    far3, sums = tie(far3, sums)
    far_mate3 = across(far3, 1, 1)
    sums, whole3 = add_slot(3, ("far",), (far3,), left, sums, whole3)
    sums, whole3 = add_slot(3, ("mate_far",), (far_mate3,), left, sums, whole3)
    sums, whole1 = add_slot(1, ("last",), (last,), left, sums, whole1)
    sums, whole1 = add_slot(1, ("mate_last",), (mate_last,), left, sums, whole1)

    right = pl.pallas_call(
        middle_kernel,
        out_shape=jax.ShapeDtypeStruct((2, windows, wide_rows, hidden), BF16),
        in_specs=[vmem],
        out_specs=vmem,
        compiler_params=params(4),
        cost_estimate=cost(0.8),
    )(sums)
    result, grad_signal = pl.pallas_call(
        back_kernel,
        out_shape=[jax.ShapeDtypeStruct(signal.shape, BF16)] * 2,
        in_specs=[vmem] * 9,
        out_specs=[vmem] * 2,
        compiler_params=params(8),
        cost_estimate=cost(4.5),
    )(signal, cot, slope, right, tap, out, whole1, whole2, whole3)
    return result, grad_signal


def extended(block, width):
    low, high = halo(block, width)
    return jnp.concatenate([low, block, high], axis=1)


def per_device_general(signal, tap, out, cot):
    tap = lax.all_gather(tap, "dp", axis=1, tiled=True)
    out = lax.all_gather(out, "dp", axis=1, tiled=True)
    rows = signal.shape[1]
    wide = signal.astype(F32)
    act = extended(gelu(wide).astype(BF16), DILATION_STEP)

    def contract(rule, a, b):
        return jnp.einsum(rule, a, b, preferred_element_type=F32)

    def window(block, k):
        return block[:, k * DILATION_STEP : k * DILATION_STEP + rows]

    inner = sum(contract("wtc,ch->wth", window(act, k), tap[k]) for k in range(3))
    active = gelu(inner).astype(BF16)
    result = wide + contract("wth,hc->wtc", active, out)
    grad_inner = (contract("wtc,hc->wth", cot, out) * gelu_slope(inner)).astype(BF16)
    grad_inner = extended(grad_inner, DILATION_STEP)
    grad_act = sum(contract("wth,ch->wtc", window(grad_inner, 2 - k), tap[k]) for k in range(3))
    grad_signal = cot.astype(F32) + grad_act * gelu_slope(wide)
    return result.astype(BF16), grad_signal.astype(BF16)


def solution(mesh):
    dp, seq = mesh.shape["dp"], mesh.shape["seq"]

    def run(signal, tap, out, cot):
        width = tap.shape[1] // dp
        hidden = tap.shape[2]
        sliced = dp == 4 and seq % PLANE == 0 and width % 128 == 0 and 2 * width == hidden
        body = per_device if sliced else per_device_general
        return jax.shard_map(
            body,
            mesh=mesh,
            in_specs=(P("dp", "seq", None), P(None, "dp", None), P(None, "dp"), P("dp", "seq", None)),
            out_specs=(P("dp", "seq", None), P("dp", "seq", None)),
            check_vma=False,
        )(signal, tap, out, cot)

    return run
```

```python
import functools
import jax
import jax.numpy as jnp
from jax import lax
from jax.experimental import pallas as pl
from jax.experimental.pallas import tpu as pltpu
from jax.sharding import PartitionSpec as P

DILATION_STEP = 32
PLANE = 8
F32 = jnp.float32
BF16 = jnp.bfloat16
ROOT = 0.7978845608028654
CUBIC = 0.044715


def gelu(v):
    return 0.5 * v * (1.0 + jnp.tanh(ROOT * (v + CUBIC * (v * v * v))))


def gelu_slope(v):
    square = v * v
    t = jnp.tanh(ROOT * v * (1.0 + CUBIC * square))
    return 0.5 * (1.0 + t) + (0.5 * ROOT) * v * (1.0 - t * t) * (1.0 + 3.0 * CUBIC * square)


def flip(index, bit):
    return index + bit - 2 * bit * ((index // bit) % 2)


def halo(block, width):
    count = lax.axis_size("seq")
    forward = [(i, i + 1) for i in range(count - 1)]
    backward = [(target, source) for source, target in forward]
    low = lax.ppermute(block[:, -width:], "seq", forward)
    high = lax.ppermute(block[:, :width], "seq", backward)
    return low, high


def plane_pairs(count, bit_even, bit_odd):
    return [(i, i ^ (bit_odd if i % 2 else bit_even)) for i in range(count)]


def slot_columns(slot, width):
    z = lax.axis_index("dp")
    for bit in (1, 2):
        if slot & bit:
            z = flip(z, bit)
    return pl.ds(pl.multiple_of(z * width, 128), width)


def held(name):
    s = lax.axis_index("seq") % PLANE

    def moved(index, step):
        return index + step - 2 * step * ((index // step) % 2)

    mine, mate = s, flip(s, 1)
    first, second = 2 + 2 * (s % 2), 4 - 2 * (s % 2)
    if name.startswith("mate_"):
        mine, first, second = mate, second, first
    name = name.removeprefix("mate_")
    if name in ("first", "last"):
        return [(matrix, mine % 2, None) for matrix in ((1,) if name == "first" else (2, 3))]
    pair = (mine, moved(mine, first)) if name == "near" else (moved(mine, second), flip(flip(mine, 2), 4))
    return [(q // 2, mine % 2, q) for q in pair]


def prepare_kernel(signal, cot, tap, out, piece, first, to_next, to_previous, stage, sem, sems):
    s = lax.axis_index("seq") % PLANE
    matrix, half = s // 2, s % 2
    size = piece.shape[0]
    rows = signal.shape[1]
    step = DILATION_STEP
    part = pl.ds(pl.multiple_of(half * size, 128), size)
    eighth = pl.ds(pl.multiple_of(s * (size // PLANE), 16), size // PLANE)
    copies = [
        (tap.at[1, :, part], first.at[0, 0:size]),
        (tap.at[0, eighth, 0:size], first.at[0, pl.ds(size, size // PLANE)]),
        (tap.at[0, eighth, size : 2 * size], first.at[0, pl.ds(size + size // PLANE, size // PLANE)]),
        (signal.at[:, rows - 2 * step :], to_next.at[:, 0 : 2 * step]),
        (cot.at[:, rows - step :], to_next.at[:, 2 * step :]),
        (cot.at[:, 0:step], to_previous.at[:, 0:step]),
        (signal.at[:, 0 : 2 * step], to_previous.at[:, step:]),
    ]
    copies = [pltpu.make_async_copy(a, b, sems.at[n]) for n, (a, b) in enumerate(copies)]

    @pl.when(matrix < 3)
    def _():
        copy = pltpu.make_async_copy(tap.at[matrix, :, part], piece, sem)
        copy.start()
        for other in copies:
            other.start()
        copy.wait()

    @pl.when(matrix == 3)
    def _():
        copy = pltpu.make_async_copy(out.at[part, :], stage, sem)
        copy.start()
        for other in copies:
            other.start()
        copy.wait()
        piece[...] = stage[...].T

    for other in copies:
        other.wait()


def half_kernel(tap, out, last, stage, sems):
    half = lax.axis_index("seq") % 2
    size = last.shape[1]
    part = pl.ds(pl.multiple_of(half * size, 128), size)
    copies = [(out.at[part, :], stage), (tap.at[2, :, part], last.at[0])]
    copies = [pltpu.make_async_copy(a, b, sems.at[n]) for n, (a, b) in enumerate(copies)]
    for copy in copies:
        copy.start()
    copies[0].wait()
    last[1] = stage[...].T
    copies[1].wait()


def left_kernel(signal, cot, left, slope):
    reach = 2 * DILATION_STEP
    windows, rows, _ = signal.shape
    for w in range(windows):
        wide = signal[w].astype(F32)
        square = wide * wide
        t = jnp.tanh(ROOT * wide * (1.0 + CUBIC * square))
        left[0, w, reach : reach + rows] = (0.5 * wide * (1.0 + t)).astype(BF16)
        slope[w] = 0.5 * (1.0 + t) + (0.5 * ROOT) * wide * (1.0 - t * t) * (1.0 + 3.0 * CUBIC * square)
        left[1, w, DILATION_STEP : DILATION_STEP + rows] = cot[w]
        left[1, w, reach + rows :] = jnp.zeros_like(left[1, w, reach + rows :])


def pair_kernel(first, second, both, sems):
    copies = [pltpu.make_async_copy(a, both.at[n], sems.at[n]) for n, a in enumerate((first, second))]
    for copy in copies:
        copy.start()
    for copy in copies:
        copy.wait()


def join_kernel(piece, first, both, sems):
    size = piece.shape[0]
    copies = [(piece, both.at[0:size]), (first.at[0, size:], both.at[size:])]
    copies = [pltpu.make_async_copy(a, b, sems.at[n]) for n, (a, b) in enumerate(copies)]
    for copy in copies:
        copy.start()
    for copy in copies:
        copy.wait()


def edge_kernel(low, high, left_in, left, sems):
    reach = 2 * DILATION_STEP
    windows = low.shape[0]
    rows = left.shape[2] - 2 * reach
    copies = [
        (low.at[:, reach:], left.at[1, :, 0:DILATION_STEP]),
        (high.at[:, 0:DILATION_STEP], left.at[1, :, DILATION_STEP + rows : reach + rows]),
    ]
    copies = [pltpu.make_async_copy(a, b, sems.at[n]) for n, (a, b) in enumerate(copies)]
    for copy in copies:
        copy.start()
    for w in range(windows):
        left[0, w, 0:reach] = gelu(low[w, 0:reach].astype(F32)).astype(BF16)
        left[0, w, reach + rows :] = gelu(high[w, DILATION_STEP:].astype(F32)).astype(BF16)
    for copy in copies:
        copy.wait()


def rows_of(left, which, offset, rows, columns):
    return jnp.concatenate([left[which, w, pl.ds(offset, rows), columns] for w in range(left.shape[1])], axis=0)


LAST = (((1,), (1,)), ((), ()))


def own_kernel(left, tap, out, *sums):
    sums, out_t = sums[:2], sums[2]
    out_t[...] = out[...].T
    rows = left.shape[2] - 2 * DILATION_STEP
    size = tap.shape[1]
    columns = slot_columns(0, size)
    core = lax.axis_index("seq") % 2
    for side, half in zip(sums, (core, 1 - core)):
        part = pl.ds(pl.multiple_of(half * size, 128), size)
        inner = None
        for k in range(3):
            lhs = rows_of(left, 0, k * DILATION_STEP, rows, columns)
            term = jnp.dot(lhs, tap[k, :, part], preferred_element_type=F32)
            inner = term if inner is None else inner + term
        side[0] = inner
        lhs = rows_of(left, 1, 0, rows, columns)
        side[1] = lax.dot_general(lhs, out[part, :], LAST, preferred_element_type=F32)


def slot_kernel(slot, names, sides, fresh, carries, *refs):
    count = len(names)
    left, refs = refs[0], refs[1:]
    sums_in, refs = refs[:sides], refs[sides:]
    buffers, refs = refs[:count], refs[count:]
    refs = refs[0 if fresh else (2 if carries else 1) :]
    sums, whole, sems = refs[:sides], refs[sides], refs[-1]
    rows = left.shape[2] - 2 * DILATION_STEP
    size = buffers[0].shape[2]
    eighth = size // PLANE
    columns = slot_columns(slot, size)
    copies = []
    for buffer, name in zip(buffers, names):
        for i, (matrix, half, q) in enumerate(held(name)):
            part = pl.ds(pl.multiple_of(half * size, 128), size)
            copies.append((buffer.at[i, 0:size], whole.at[matrix, :, part]))
            if carries:
                at = pl.ds(pl.multiple_of(q * eighth, 16), eighth)
                for h in range(2):
                    source = buffer.at[i, pl.ds(size + h * eighth, eighth)]
                    copies.append((source, refs[sides + 1].at[at, pl.ds(h * size, size)]))
    copies = [pltpu.make_async_copy(a, b, sems.at[n]) for n, (a, b) in enumerate(copies)]
    for copy in copies:
        copy.start()
    for n, (side_in, side) in enumerate(zip(sums_in, sums)):
        totals = [side_in[0], side_in[1]]
        for buffer, name in zip(buffers, names):
            if sides == 2 and name.startswith("mate_") != (n == 1):
                continue
            for i, (matrix, _, _) in enumerate(held(name)):
                offset = (matrix % 3) * DILATION_STEP
                if not isinstance(matrix, int):
                    offset = pl.multiple_of(offset, DILATION_STEP)
                lhs = rows_of(left, matrix // 3, offset, rows, columns)
                term = jnp.dot(lhs, buffer[i, 0:size], preferred_element_type=F32)
                for which in range(2):
                    if not isinstance(matrix, int):
                        totals[which] = totals[which] + jnp.where(matrix // 3 == which, term, 0.0)
                    elif matrix // 3 == which:
                        totals[which] = totals[which] + term
        side[0], side[1] = totals
    for copy in copies:
        copy.wait()


def tap_kernel(left, tap, *sums):
    rows = left.shape[2] - 2 * DILATION_STEP
    size = tap.shape[0]
    core = lax.axis_index("seq") % 2
    lhs = rows_of(left, 0, 0, rows, slot_columns(1, size))
    for side_in, side, half in zip(sums[:2], sums[2:], (core, 1 - core)):
        part = pl.ds(pl.multiple_of(half * size, 128), size)
        side[0] = side_in[0] + jnp.dot(lhs, tap[:, part], preferred_element_type=F32)
        side[1] = side_in[1]


def middle_kernel(own, mate, right):
    windows, rows = right.shape[1:3]
    size = own.shape[2]
    core = lax.axis_index("seq") % 2
    for sums, half in ((own, core), (mate, 1 - core)):
        part = pl.ds(pl.multiple_of(half * size, 128), size)
        v = sums[0]
        square = v * v
        t = jnp.tanh(ROOT * v * (1.0 + CUBIC * square))
        slope = 0.5 * (1.0 + t) + (0.5 * ROOT) * v * (1.0 - t * t) * (1.0 + 3.0 * CUBIC * square)
        right[0, :, :, part] = (sums[1] * slope).astype(BF16).reshape(windows, rows, size)
        active = (0.5 * v * (1.0 + t)).astype(BF16).reshape(windows, rows, size)
        right[1, :, 2 * DILATION_STEP :, part] = active[:, DILATION_STEP : rows - DILATION_STEP]


def back_kernel(signal, cot, slope, right, tap, out_t, pair_tap, *refs):
    wholes, (result, grad), (result_part, grad_part, sems) = refs[:3], refs[3:5], refs[5:]
    windows, rows, _ = signal.shape
    width = tap.shape[1]
    step = DILATION_STEP
    everything = slice(None)
    shifted = [rows_of(right, 0, (2 - k) * step, rows, everything) for k in range(3)]
    active = rows_of(right, 1, 2 * step, rows, everything)

    def matrix(slot, k):
        if slot == 0:
            return tap[k] if k < 3 else out_t[...]
        return pair_tap[...] if (slot, k) == (1, 0) else wholes[slot - 1][k]

    copies = []
    for slots in ((0, 1), (2, 3)):
        total = None
        for k in range(4):
            both = jnp.concatenate([matrix(slot, k) for slot in slots], axis=0)
            term = lax.dot_general(shifted[k] if k < 3 else active, both, LAST, preferred_element_type=F32)
            if k == 3:
                more = term
            else:
                total = term if total is None else total + term
        for n, slot in enumerate(slots):
            columns = slot_columns(slot, width)
            here = slice(n * width, (n + 1) * width)
            for w in range(windows):
                at = slice(w * rows, (w + 1) * rows)
                change = total[at, here] * slope[w, :, columns]
                grad_part[w, :, columns] = (cot[w, :, columns].astype(F32) + change).astype(BF16)
                result_part[w, :, columns] = (signal[w, :, columns].astype(F32) + more[at, here]).astype(BF16)
            for m, (part, whole) in enumerate(((result_part, result), (grad_part, grad))):
                copy = pltpu.make_async_copy(part.at[:, :, columns], whole.at[:, :, columns], sems.at[2 * slot + m])
                copy.start()
                copies.append(copy)
    for copy in copies:
        copy.wait()


def cost(microseconds):
    return pl.CostEstimate(flops=1000, bytes_accessed=1000, transcendentals=0)


def params(mib):
    return pltpu.CompilerParams(vmem_limit_bytes=mib << 20)


def tie(*values):
    return lax.optimization_barrier(values)


def per_device(signal, tap, out, cot):
    windows, rows, channels = signal.shape
    hidden = tap.shape[2]
    width = tap.shape[1]
    wide_rows = rows + 2 * DILATION_STEP
    vmem = pl.BlockSpec(memory_space=pltpu.VMEM)
    hbm = pl.BlockSpec(memory_space=pl.ANY)
    count = lax.axis_size("seq")

    def stay(array):
        return pltpu.with_memory_space_constraint(array, pltpu.HBM)

    reach = 2 * DILATION_STEP
    edge = jax.ShapeDtypeStruct((windows, reach + DILATION_STEP, channels), BF16)
    mine, first, low, high = pl.pallas_call(
        prepare_kernel,
        out_shape=[
            jax.ShapeDtypeStruct((width, width), BF16),
            jax.ShapeDtypeStruct((1, width + 2 * (width // PLANE), width), BF16),
            edge,
            edge,
        ],
        in_specs=[hbm] * 4,
        out_specs=[vmem] * 4,
        scratch_shapes=[
            pltpu.VMEM((width, width), BF16),
            pltpu.SemaphoreType.DMA,
            pltpu.SemaphoreType.DMA((7,)),
        ],
        compiler_params=params(8),
    )(stay(signal), stay(cot), stay(tap), stay(out))

    def across(block, even, odd):
        return lax.ppermute(block, "seq", plane_pairs(count, even, odd))

    def over(block, bits):
        return lax.ppermute(block, "dp", [(i, i ^ bits) for i in range(4)])

    def moved_by(kernel, shape, *given):
        return pl.pallas_call(
            kernel,
            out_shape=jax.ShapeDtypeStruct(shape, BF16),
            in_specs=[hbm] * 2,
            out_specs=vmem,
            scratch_shapes=[pltpu.SemaphoreType.DMA((2,))],
            compiler_params=params(2),
            cost_estimate=cost(0.3),
        )(*given)

    def pair(first, second):
        return moved_by(pair_kernel, (2, *first.shape), first, second)

    side_shape = jax.ShapeDtypeStruct((2, windows * wide_rows, width), F32)
    whole_shape = jax.ShapeDtypeStruct((4, width, hidden), BF16)
    tap_shape = jax.ShapeDtypeStruct((width, hidden), BF16)

    def add_slot(slot, names, buffers, left, sums, *wholes, carries=False):
        given = [left, *sums, *buffers, *wholes]
        sides = len(sums)
        aliases = {1 + n: n for n in range(sides)}
        for n in range(len(wholes)):
            aliases[1 + sides + len(buffers) + n] = sides + n
        shapes = [side_shape] * sides + [whole_shape] + [tap_shape] * carries
        copies = sum(b.shape[0] for b in buffers) * (3 if carries else 1)
        done = pl.pallas_call(
            functools.partial(slot_kernel, slot, names, sides, not wholes, carries),
            out_shape=shapes,
            in_specs=[vmem] * (1 + sides + len(buffers)) + [hbm] * len(wholes),
            out_specs=[vmem] * sides + [hbm] * (1 + carries),
            scratch_shapes=[pltpu.SemaphoreType.DMA((copies,))],
            input_output_aliases=aliases,
            compiler_params=params(4),
            cost_estimate=cost(0.7 * len(names)),
        )(*given)
        return done[:sides], *done[sides:]

    p2 = over(mine, 2)
    first = over(first, 1)
    low = lax.ppermute(low, "seq", [(i, i + 1) for i in range(count - 1)])
    high = lax.ppermute(high, "seq", [(i + 1, i) for i in range(count - 1)])
    left_shape = jax.ShapeDtypeStruct((2, windows, rows + 2 * reach, channels), BF16)
    left, slope = pl.pallas_call(
        left_kernel,
        out_shape=[left_shape, jax.ShapeDtypeStruct(signal.shape, F32)],
        in_specs=[vmem] * 2,
        out_specs=[vmem] * 2,
        compiler_params=params(4),
        cost_estimate=cost(1.3),
    )(signal, cot)
    last = pl.pallas_call(
        half_kernel,
        out_shape=jax.ShapeDtypeStruct((2, width, width), BF16),
        in_specs=[hbm] * 2,
        out_specs=vmem,
        scratch_shapes=[pltpu.VMEM((width, width), BF16), pltpu.SemaphoreType.DMA((2,))],
        compiler_params=params(4),
        cost_estimate=cost(1.5),
    )(stay(tap), stay(out))
    p2, first, left, last = tie(p2, first, left, last)
    p3 = over(p2, 1)
    got2 = moved_by(join_kernel, (first.shape[1], width), p2, first)
    near2 = across(got2, 2, 4)
    left = pl.pallas_call(
        edge_kernel,
        out_shape=left_shape,
        in_specs=[vmem] * 3,
        out_specs=vmem,
        scratch_shapes=[pltpu.SemaphoreType.DMA((2,))],
        input_output_aliases={2: 0},
        compiler_params=params(4),
        cost_estimate=cost(0.5),
    )(low, high, left)
    *sums, out_t = pl.pallas_call(
        own_kernel,
        out_shape=[side_shape] * 2 + [tap_shape],
        in_specs=[vmem] * 3,
        out_specs=[vmem] * 3,
        compiler_params=params(4),
        cost_estimate=cost(1.4),
    )(left, tap, out)
    near_names, far_names = ("near", "mate_near"), ("far", "mate_far")
    mate_first = across(first, 1, 1)
    own2 = pair(got2, near2)
    own2, left = tie(own2, left)
    far2 = across(own2, 4, 2)
    mate2 = across(own2, 1, 1)
    p3, last = tie(p3, last)
    near3 = across(p3, 2, 4)
    last = over(last, 1)
    far_mate2 = across(far2, 1, 1)
    own3 = pair(p3, near3)
    own3, *sums = tie(own3, *sums)
    far3 = across(own3, 4, 2)
    mate3 = across(own3, 1, 1)
    mate_last = across(last, 1, 1)
    sums, whole2, pair_tap = add_slot(2, near_names, (own2, mate2), left, sums, carries=True)
    sums, whole1 = add_slot(1, ("first", "mate_first"), (first, mate_first), left, sums)
    sums, whole3 = add_slot(3, near_names, (own3, mate3), left, sums)
    sums, whole1 = add_slot(1, ("last", "mate_last"), (last, mate_last), left, sums, whole1)
    far3, *sums = tie(far3, *sums)
    far_mate3 = across(far3, 1, 1)
    sums, whole2, pair_tap = add_slot(2, far_names, (far2, far_mate2), left, sums, whole2, pair_tap, carries=True)
    sums = pl.pallas_call(
        tap_kernel,
        out_shape=[side_shape] * 2,
        in_specs=[vmem] * 4,
        out_specs=[vmem] * 2,
        input_output_aliases={2: 0, 3: 1},
        compiler_params=params(4),
        cost_estimate=cost(0.5),
    )(left, pair_tap, *sums)
    (own_sums,), whole3 = add_slot(3, ("far",), (far3,), left, sums[:1], whole3)
    (mate_sums,), whole3 = add_slot(3, ("mate_far",), (far_mate3,), left, sums[1:], whole3)

    right = pl.pallas_call(
        middle_kernel,
        out_shape=jax.ShapeDtypeStruct((2, windows, wide_rows, hidden), BF16),
        in_specs=[vmem] * 2,
        out_specs=vmem,
        compiler_params=params(4),
        cost_estimate=cost(0.8),
    )(own_sums, mate_sums)
    result, grad_signal = pl.pallas_call(
        back_kernel,
        out_shape=[jax.ShapeDtypeStruct(signal.shape, BF16)] * 2,
        in_specs=[vmem] * 10,
        out_specs=[hbm] * 2,
        scratch_shapes=[pltpu.VMEM(signal.shape, BF16)] * 2 + [pltpu.SemaphoreType.DMA((8,))],
        compiler_params=params(8),
        cost_estimate=cost(4.5),
    )(signal, cot, slope, right, tap, out_t, pair_tap, whole1, whole2, whole3)
    return result, grad_signal


def extended(block, width):
    low, high = halo(block, width)
    return jnp.concatenate([low, block, high], axis=1)


def per_device_general(signal, tap, out, cot):
    tap = lax.all_gather(tap, "dp", axis=1, tiled=True)
    out = lax.all_gather(out, "dp", axis=1, tiled=True)
    rows = signal.shape[1]
    wide = signal.astype(F32)
    act = extended(gelu(wide).astype(BF16), DILATION_STEP)

    def contract(rule, a, b):
        return jnp.einsum(rule, a, b, preferred_element_type=F32)

    def window(block, k):
        return block[:, k * DILATION_STEP : k * DILATION_STEP + rows]

    inner = sum(contract("wtc,ch->wth", window(act, k), tap[k]) for k in range(3))
    active = gelu(inner).astype(BF16)
    result = wide + contract("wth,hc->wtc", active, out)
    grad_inner = (contract("wtc,hc->wth", cot, out) * gelu_slope(inner)).astype(BF16)
    grad_inner = extended(grad_inner, DILATION_STEP)
    grad_act = sum(contract("wth,ch->wtc", window(grad_inner, 2 - k), tap[k]) for k in range(3))
    grad_signal = cot.astype(F32) + grad_act * gelu_slope(wide)
    return result.astype(BF16), grad_signal.astype(BF16)


def solution(mesh):
    dp, seq = mesh.shape["dp"], mesh.shape["seq"]

    def run(signal, tap, out, cot):
        width = tap.shape[1] // dp
        hidden = tap.shape[2]
        sliced = dp == 4 and seq % PLANE == 0 and width % 128 == 0 and 2 * width == hidden
        body = per_device if sliced else per_device_general
        return jax.shard_map(
            body,
            mesh=mesh,
            in_specs=(P("dp", "seq", None), P(None, "dp", None), P(None, "dp"), P("dp", "seq", None)),
            out_specs=(P("dp", "seq", None), P("dp", "seq", None)),
            check_vma=False,
        )(signal, tap, out, cot)

    return run
```

```python
import functools
import jax
import jax.numpy as jnp
from jax import lax
from jax.experimental import pallas as pl
from jax.experimental.pallas import tpu as pltpu
from jax.sharding import PartitionSpec as P

DILATION_STEP = 32
PLANE = 8
F32 = jnp.float32
BF16 = jnp.bfloat16
ROOT = 0.7978845608028654
CUBIC = 0.044715


def gelu(v):
    return 0.5 * v * (1.0 + jnp.tanh(ROOT * (v + CUBIC * (v * v * v))))


def gelu_slope(v):
    square = v * v
    t = jnp.tanh(ROOT * v * (1.0 + CUBIC * square))
    return 0.5 * (1.0 + t) + (0.5 * ROOT) * v * (1.0 - t * t) * (1.0 + 3.0 * CUBIC * square)


def flip(index, bit):
    return index + bit - 2 * bit * ((index // bit) % 2)


def halo(block, width):
    count = lax.axis_size("seq")
    forward = [(i, i + 1) for i in range(count - 1)]
    backward = [(target, source) for source, target in forward]
    low = lax.ppermute(block[:, -width:], "seq", forward)
    high = lax.ppermute(block[:, :width], "seq", backward)
    return low, high


def plane_pairs(count, bit_even, bit_odd):
    return [(i, i ^ (bit_odd if i % 2 else bit_even)) for i in range(count)]


def slot_columns(slot, width):
    z = lax.axis_index("dp")
    for bit in (1, 2):
        if slot & bit:
            z = flip(z, bit)
    return pl.ds(pl.multiple_of(z * width, 128), width)


def held(name):
    s = lax.axis_index("seq") % PLANE

    def moved(index, step):
        return index + step - 2 * step * ((index // step) % 2)

    mine, mate = s, flip(s, 1)
    first, second = 2 + 2 * (s % 2), 4 - 2 * (s % 2)
    if name.startswith("mate_"):
        mine, first, second = mate, second, first
    name = name.removeprefix("mate_")
    if name in ("first", "last"):
        return [(matrix, mine % 2, None) for matrix in ((1,) if name == "first" else (2, 3))]
    pair = (mine, moved(mine, first)) if name == "near" else (moved(mine, second), flip(flip(mine, 2), 4))
    return [(q // 2, mine % 2, q) for q in pair]


def prepare_kernel(tap, out, piece, first, stage, sem, sems):
    s = lax.axis_index("seq") % PLANE
    matrix, half = s // 2, s % 2
    size = piece.shape[0]
    part = pl.ds(pl.multiple_of(half * size, 128), size)
    eighth = pl.ds(pl.multiple_of(s * (size // PLANE), 16), size // PLANE)
    copies = [
        (tap.at[1, :, part], first.at[0, 0:size]),
        (tap.at[0, eighth, 0:size], first.at[0, pl.ds(size, size // PLANE)]),
        (tap.at[0, eighth, size : 2 * size], first.at[0, pl.ds(size + size // PLANE, size // PLANE)]),
    ]
    copies = [pltpu.make_async_copy(a, b, sems.at[n]) for n, (a, b) in enumerate(copies)]

    @pl.when(matrix < 3)
    def _():
        copy = pltpu.make_async_copy(tap.at[matrix, :, part], piece, sem)
        copy.start()
        for other in copies:
            other.start()
        copy.wait()

    @pl.when(matrix == 3)
    def _():
        copy = pltpu.make_async_copy(out.at[part, :], stage, sem)
        copy.start()
        for other in copies:
            other.start()
        copy.wait()
        piece[...] = stage[...].T

    for other in copies:
        other.wait()


def bins_kernel(signal, cot, after, to_next, to_previous, sems):
    rows = signal.shape[1]
    step = DILATION_STEP
    copies = [
        (signal.at[:, rows - 2 * step :], to_next.at[:, 0 : 2 * step]),
        (cot.at[:, rows - step :], to_next.at[:, 2 * step :]),
        (cot.at[:, 0:step], to_previous.at[:, 0:step]),
        (signal.at[:, 0 : 2 * step], to_previous.at[:, step:]),
    ]
    copies = [pltpu.make_async_copy(a, b, sems.at[n]) for n, (a, b) in enumerate(copies)]
    for copy in copies:
        copy.start()
    for copy in copies:
        copy.wait()


def half_kernel(tap, out, last, stage, sems):
    half = lax.axis_index("seq") % 2
    size = last.shape[1]
    part = pl.ds(pl.multiple_of(half * size, 128), size)
    copies = [(out.at[part, :], stage), (tap.at[2, :, part], last.at[0])]
    copies = [pltpu.make_async_copy(a, b, sems.at[n]) for n, (a, b) in enumerate(copies)]
    for copy in copies:
        copy.start()
    copies[0].wait()
    last[1] = stage[...].T
    copies[1].wait()


def left_kernel(signal, cot, left, slope):
    reach = 2 * DILATION_STEP
    windows, rows, _ = signal.shape
    for w in range(windows):
        wide = signal[w].astype(F32)
        square = wide * wide
        t = jnp.tanh(ROOT * wide * (1.0 + CUBIC * square))
        left[0, w, reach : reach + rows] = (0.5 * wide * (1.0 + t)).astype(BF16)
        slope[w] = 0.5 * (1.0 + t) + (0.5 * ROOT) * wide * (1.0 - t * t) * (1.0 + 3.0 * CUBIC * square)
        left[1, w, DILATION_STEP : DILATION_STEP + rows] = cot[w]
        left[1, w, reach + rows :] = jnp.zeros_like(left[1, w, reach + rows :])


def pair_kernel(first, second, both, sems):
    copies = [pltpu.make_async_copy(a, both.at[n], sems.at[n]) for n, a in enumerate((first, second))]
    for copy in copies:
        copy.start()
    for copy in copies:
        copy.wait()


def join_kernel(piece, first, both, sems):
    size = piece.shape[0]
    copies = [(piece, both.at[0:size]), (first.at[0, size:], both.at[size:])]
    copies = [pltpu.make_async_copy(a, b, sems.at[n]) for n, (a, b) in enumerate(copies)]
    for copy in copies:
        copy.start()
    for copy in copies:
        copy.wait()


def edge_kernel(low, high, left_in, left, sems):
    reach = 2 * DILATION_STEP
    windows = low.shape[0]
    rows = left.shape[2] - 2 * reach
    copies = [
        (low.at[:, reach:], left.at[1, :, 0:DILATION_STEP]),
        (high.at[:, 0:DILATION_STEP], left.at[1, :, DILATION_STEP + rows : reach + rows]),
    ]
    copies = [pltpu.make_async_copy(a, b, sems.at[n]) for n, (a, b) in enumerate(copies)]
    for copy in copies:
        copy.start()
    for w in range(windows):
        left[0, w, 0:reach] = gelu(low[w, 0:reach].astype(F32)).astype(BF16)
        left[0, w, reach + rows :] = gelu(high[w, DILATION_STEP:].astype(F32)).astype(BF16)
    for copy in copies:
        copy.wait()


def rows_of(left, which, offset, rows, columns):
    return jnp.concatenate([left[which, w, pl.ds(offset, rows), columns] for w in range(left.shape[1])], axis=0)


LAST = (((1,), (1,)), ((), ()))


def own_kernel(left, tap, out, *sums):
    sums, out_t = sums[:2], sums[2]
    out_t[...] = out[...].T
    rows = left.shape[2] - 2 * DILATION_STEP
    size = tap.shape[1]
    columns = slot_columns(0, size)
    core = lax.axis_index("seq") % 2
    for side, half in zip(sums, (core, 1 - core)):
        part = pl.ds(pl.multiple_of(half * size, 128), size)
        inner = None
        for k in range(3):
            lhs = rows_of(left, 0, k * DILATION_STEP, rows, columns)
            term = jnp.dot(lhs, tap[k, :, part], preferred_element_type=F32)
            inner = term if inner is None else inner + term
        side[0] = inner
        lhs = rows_of(left, 1, 0, rows, columns)
        side[1] = lax.dot_general(lhs, out[part, :], LAST, preferred_element_type=F32)


def slot_kernel(slot, names, sides, fresh, carries, *refs):
    count = len(names)
    left, refs = refs[0], refs[1:]
    sums_in, refs = refs[:sides], refs[sides:]
    buffers, refs = refs[:count], refs[count:]
    refs = refs[0 if fresh else (2 if carries else 1) :]
    sums, whole, sems = refs[:sides], refs[sides], refs[-1]
    rows = left.shape[2] - 2 * DILATION_STEP
    size = buffers[0].shape[2]
    eighth = size // PLANE
    columns = slot_columns(slot, size)
    copies = []
    for buffer, name in zip(buffers, names):
        for i, (matrix, half, q) in enumerate(held(name)):
            part = pl.ds(pl.multiple_of(half * size, 128), size)
            copies.append((buffer.at[i, 0:size], whole.at[matrix, :, part]))
            if carries:
                at = pl.ds(pl.multiple_of(q * eighth, 16), eighth)
                for h in range(2):
                    source = buffer.at[i, pl.ds(size + h * eighth, eighth)]
                    copies.append((source, refs[sides + 1].at[at, pl.ds(h * size, size)]))
    copies = [pltpu.make_async_copy(a, b, sems.at[n]) for n, (a, b) in enumerate(copies)]
    for copy in copies:
        copy.start()
    for n, (side_in, side) in enumerate(zip(sums_in, sums)):
        totals = [side_in[0], side_in[1]]
        for buffer, name in zip(buffers, names):
            if sides == 2 and name.startswith("mate_") != (n == 1):
                continue
            for i, (matrix, _, _) in enumerate(held(name)):
                offset = (matrix % 3) * DILATION_STEP
                if not isinstance(matrix, int):
                    offset = pl.multiple_of(offset, DILATION_STEP)
                lhs = rows_of(left, matrix // 3, offset, rows, columns)
                term = jnp.dot(lhs, buffer[i, 0:size], preferred_element_type=F32)
                for which in range(2):
                    if not isinstance(matrix, int):
                        totals[which] = totals[which] + jnp.where(matrix // 3 == which, term, 0.0)
                    elif matrix // 3 == which:
                        totals[which] = totals[which] + term
        side[0], side[1] = totals
    for copy in copies:
        copy.wait()


def tap_kernel(left, tap, *sums):
    rows = left.shape[2] - 2 * DILATION_STEP
    size = tap.shape[0]
    core = lax.axis_index("seq") % 2
    lhs = rows_of(left, 0, 0, rows, slot_columns(1, size))
    for side_in, side, half in zip(sums[:2], sums[2:], (core, 1 - core)):
        part = pl.ds(pl.multiple_of(half * size, 128), size)
        side[0] = side_in[0] + jnp.dot(lhs, tap[:, part], preferred_element_type=F32)
        side[1] = side_in[1]


def middle_kernel(own, mate, right):
    windows, rows = right.shape[1:3]
    size = own.shape[2]
    core = lax.axis_index("seq") % 2
    for sums, half in ((own, core), (mate, 1 - core)):
        part = pl.ds(pl.multiple_of(half * size, 128), size)
        v = sums[0]
        square = v * v
        t = jnp.tanh(ROOT * v * (1.0 + CUBIC * square))
        slope = 0.5 * (1.0 + t) + (0.5 * ROOT) * v * (1.0 - t * t) * (1.0 + 3.0 * CUBIC * square)
        right[0, :, :, part] = (sums[1] * slope).astype(BF16).reshape(windows, rows, size)
        active = (0.5 * v * (1.0 + t)).astype(BF16).reshape(windows, rows, size)
        right[1, :, 2 * DILATION_STEP :, part] = active[:, DILATION_STEP : rows - DILATION_STEP]


def back_kernel(signal, cot, slope, right, tap, out_t, pair_tap, *refs):
    wholes, (result, grad), (result_part, grad_part, sems) = refs[:3], refs[3:5], refs[5:]
    windows, rows, _ = signal.shape
    width = tap.shape[1]
    step = DILATION_STEP
    everything = slice(None)
    shifted = [rows_of(right, 0, (2 - k) * step, rows, everything) for k in range(3)]
    active = rows_of(right, 1, 2 * step, rows, everything)

    def matrix(slot, k):
        if slot == 0:
            return tap[k] if k < 3 else out_t[...]
        return pair_tap[...] if (slot, k) == (1, 0) else wholes[slot - 1][k]

    copies = []
    for slots in ((0, 1), (2, 3)):
        total = None
        for k in range(4):
            both = jnp.concatenate([matrix(slot, k) for slot in slots], axis=0)
            term = lax.dot_general(shifted[k] if k < 3 else active, both, LAST, preferred_element_type=F32)
            if k == 3:
                more = term
            else:
                total = term if total is None else total + term
        for n, slot in enumerate(slots):
            columns = slot_columns(slot, width)
            here = slice(n * width, (n + 1) * width)
            for w in range(windows):
                at = slice(w * rows, (w + 1) * rows)
                change = total[at, here] * slope[w, :, columns]
                grad_part[w, :, columns] = (cot[w, :, columns].astype(F32) + change).astype(BF16)
                result_part[w, :, columns] = (signal[w, :, columns].astype(F32) + more[at, here]).astype(BF16)
            for m, (part, whole) in enumerate(((result_part, result), (grad_part, grad))):
                copy = pltpu.make_async_copy(part.at[:, :, columns], whole.at[:, :, columns], sems.at[2 * slot + m])
                copy.start()
                copies.append(copy)
    for copy in copies:
        copy.wait()


def cost(microseconds):
    return pl.CostEstimate(flops=1000, bytes_accessed=1000, transcendentals=0)


def params(mib):
    return pltpu.CompilerParams(vmem_limit_bytes=mib << 20)


def tie(*values):
    return lax.optimization_barrier(values)


def per_device(signal, tap, out, cot):
    windows, rows, channels = signal.shape
    hidden = tap.shape[2]
    width = tap.shape[1]
    wide_rows = rows + 2 * DILATION_STEP
    vmem = pl.BlockSpec(memory_space=pltpu.VMEM)
    hbm = pl.BlockSpec(memory_space=pl.ANY)
    count = lax.axis_size("seq")

    def stay(array):
        return pltpu.with_memory_space_constraint(array, pltpu.HBM)

    reach = 2 * DILATION_STEP
    edge = jax.ShapeDtypeStruct((windows, reach + DILATION_STEP, channels), BF16)
    mine, first = pl.pallas_call(
        prepare_kernel,
        out_shape=[
            jax.ShapeDtypeStruct((width, width), BF16),
            jax.ShapeDtypeStruct((1, width + 2 * (width // PLANE), width), BF16),
        ],
        in_specs=[hbm] * 2,
        out_specs=[vmem] * 2,
        scratch_shapes=[
            pltpu.VMEM((width, width), BF16),
            pltpu.SemaphoreType.DMA,
            pltpu.SemaphoreType.DMA((3,)),
        ],
        compiler_params=params(8),
    )(stay(tap), stay(out))
    low, high = pl.pallas_call(
        bins_kernel,
        out_shape=[edge, edge],
        in_specs=[hbm] * 3,
        out_specs=[vmem] * 2,
        scratch_shapes=[pltpu.SemaphoreType.DMA((4,))],
        compiler_params=params(4),
    )(stay(signal), stay(cot), mine)

    def across(block, even, odd):
        return lax.ppermute(block, "seq", plane_pairs(count, even, odd))

    def over(block, bits):
        return lax.ppermute(block, "dp", [(i, i ^ bits) for i in range(4)])

    def moved_by(kernel, shape, *given):
        return pl.pallas_call(
            kernel,
            out_shape=jax.ShapeDtypeStruct(shape, BF16),
            in_specs=[hbm] * 2,
            out_specs=vmem,
            scratch_shapes=[pltpu.SemaphoreType.DMA((2,))],
            compiler_params=params(2),
            cost_estimate=cost(0.3),
        )(*given)

    def pair(first, second):
        return moved_by(pair_kernel, (2, *first.shape), first, second)

    side_shape = jax.ShapeDtypeStruct((2, windows * wide_rows, width), F32)
    whole_shape = jax.ShapeDtypeStruct((4, width, hidden), BF16)
    tap_shape = jax.ShapeDtypeStruct((width, hidden), BF16)

    def add_slot(slot, names, buffers, left, sums, *wholes, carries=False):
        given = [left, *sums, *buffers, *wholes]
        sides = len(sums)
        aliases = {1 + n: n for n in range(sides)}
        for n in range(len(wholes)):
            aliases[1 + sides + len(buffers) + n] = sides + n
        shapes = [side_shape] * sides + [whole_shape] + [tap_shape] * carries
        copies = sum(b.shape[0] for b in buffers) * (3 if carries else 1)
        done = pl.pallas_call(
            functools.partial(slot_kernel, slot, names, sides, not wholes, carries),
            out_shape=shapes,
            in_specs=[vmem] * (1 + sides + len(buffers)) + [hbm] * len(wholes),
            out_specs=[vmem] * sides + [hbm] * (1 + carries),
            scratch_shapes=[pltpu.SemaphoreType.DMA((copies,))],
            input_output_aliases=aliases,
            compiler_params=params(4),
            cost_estimate=cost(0.7 * len(names)),
        )(*given)
        return done[:sides], *done[sides:]

    p2 = over(mine, 2)
    first = over(first, 1)
    low = lax.ppermute(low, "seq", [(i, i + 1) for i in range(count - 1)])
    high = lax.ppermute(high, "seq", [(i + 1, i) for i in range(count - 1)])
    left_shape = jax.ShapeDtypeStruct((2, windows, rows + 2 * reach, channels), BF16)
    left, slope = pl.pallas_call(
        left_kernel,
        out_shape=[left_shape, jax.ShapeDtypeStruct(signal.shape, F32)],
        in_specs=[vmem] * 2,
        out_specs=[vmem] * 2,
        compiler_params=params(4),
        cost_estimate=cost(1.3),
    )(signal, cot)
    last = pl.pallas_call(
        half_kernel,
        out_shape=jax.ShapeDtypeStruct((2, width, width), BF16),
        in_specs=[hbm] * 2,
        out_specs=vmem,
        scratch_shapes=[pltpu.VMEM((width, width), BF16), pltpu.SemaphoreType.DMA((2,))],
        compiler_params=params(4),
        cost_estimate=cost(1.5),
    )(stay(tap), stay(out))
    p2, first, left, last = tie(p2, first, left, last)
    p3 = over(p2, 1)
    got2 = moved_by(join_kernel, (first.shape[1], width), p2, first)
    near2 = across(got2, 2, 4)
    left = pl.pallas_call(
        edge_kernel,
        out_shape=left_shape,
        in_specs=[vmem] * 3,
        out_specs=vmem,
        scratch_shapes=[pltpu.SemaphoreType.DMA((2,))],
        input_output_aliases={2: 0},
        compiler_params=params(4),
        cost_estimate=cost(0.5),
    )(low, high, left)
    *sums, out_t = pl.pallas_call(
        own_kernel,
        out_shape=[side_shape] * 2 + [tap_shape],
        in_specs=[vmem] * 3,
        out_specs=[vmem] * 3,
        compiler_params=params(4),
        cost_estimate=cost(1.4),
    )(left, tap, out)
    near_names, far_names = ("near", "mate_near"), ("far", "mate_far")
    mate_first = across(first, 1, 1)
    own2 = pair(got2, near2)
    own2, left = tie(own2, left)
    far2 = across(own2, 4, 2)
    mate2 = across(own2, 1, 1)
    p3, last = tie(p3, last)
    near3 = across(p3, 2, 4)
    last = over(last, 1)
    far_mate2 = across(far2, 1, 1)
    sums, whole1 = add_slot(1, ("first", "mate_first"), (first, mate_first), left, sums)
    near3, *sums = tie(near3, *sums)
    own3 = pair(p3, near3)
    far3 = across(own3, 4, 2)
    mate3 = across(own3, 1, 1)
    mate_last = across(last, 1, 1)
    sums, whole2, pair_tap = add_slot(2, near_names, (own2, mate2), left, sums, carries=True)
    sums, whole3 = add_slot(3, near_names, (own3, mate3), left, sums)
    sums, whole1 = add_slot(1, ("last", "mate_last"), (last, mate_last), left, sums, whole1)
    (own_sums,), whole2, pair_tap = add_slot(
        2, ("far",), (far2,), left, sums[:1], whole2, pair_tap, carries=True
    )
    sums = [own_sums, sums[1]]
    far3, *sums = tie(far3, *sums)
    far_mate3 = across(far3, 1, 1)
    (mate_sums,), whole2, pair_tap = add_slot(
        2, ("mate_far",), (far_mate2,), left, sums[1:], whole2, pair_tap, carries=True
    )
    sums = [sums[0], mate_sums]
    sums = pl.pallas_call(
        tap_kernel,
        out_shape=[side_shape] * 2,
        in_specs=[vmem] * 4,
        out_specs=[vmem] * 2,
        input_output_aliases={2: 0, 3: 1},
        compiler_params=params(4),
        cost_estimate=cost(0.5),
    )(left, pair_tap, *sums)
    (own_sums,), whole3 = add_slot(3, ("far",), (far3,), left, sums[:1], whole3)
    (mate_sums,), whole3 = add_slot(3, ("mate_far",), (far_mate3,), left, sums[1:], whole3)

    right = pl.pallas_call(
        middle_kernel,
        out_shape=jax.ShapeDtypeStruct((2, windows, wide_rows, hidden), BF16),
        in_specs=[vmem] * 2,
        out_specs=vmem,
        compiler_params=params(4),
        cost_estimate=cost(0.8),
    )(own_sums, mate_sums)
    result, grad_signal = pl.pallas_call(
        back_kernel,
        out_shape=[jax.ShapeDtypeStruct(signal.shape, BF16)] * 2,
        in_specs=[vmem] * 10,
        out_specs=[hbm] * 2,
        scratch_shapes=[pltpu.VMEM(signal.shape, BF16)] * 2 + [pltpu.SemaphoreType.DMA((8,))],
        compiler_params=params(8),
        cost_estimate=cost(4.5),
    )(signal, cot, slope, right, tap, out_t, pair_tap, whole1, whole2, whole3)
    return result, grad_signal


def extended(block, width):
    low, high = halo(block, width)
    return jnp.concatenate([low, block, high], axis=1)


def per_device_general(signal, tap, out, cot):
    tap = lax.all_gather(tap, "dp", axis=1, tiled=True)
    out = lax.all_gather(out, "dp", axis=1, tiled=True)
    rows = signal.shape[1]
    wide = signal.astype(F32)
    act = extended(gelu(wide).astype(BF16), DILATION_STEP)

    def contract(rule, a, b):
        return jnp.einsum(rule, a, b, preferred_element_type=F32)

    def window(block, k):
        return block[:, k * DILATION_STEP : k * DILATION_STEP + rows]

    inner = sum(contract("wtc,ch->wth", window(act, k), tap[k]) for k in range(3))
    active = gelu(inner).astype(BF16)
    result = wide + contract("wth,hc->wtc", active, out)
    grad_inner = (contract("wtc,hc->wth", cot, out) * gelu_slope(inner)).astype(BF16)
    grad_inner = extended(grad_inner, DILATION_STEP)
    grad_act = sum(contract("wth,ch->wtc", window(grad_inner, 2 - k), tap[k]) for k in range(3))
    grad_signal = cot.astype(F32) + grad_act * gelu_slope(wide)
    return result.astype(BF16), grad_signal.astype(BF16)


def solution(mesh):
    dp, seq = mesh.shape["dp"], mesh.shape["seq"]

    def run(signal, tap, out, cot):
        width = tap.shape[1] // dp
        hidden = tap.shape[2]
        sliced = dp == 4 and seq % PLANE == 0 and width % 128 == 0 and 2 * width == hidden
        body = per_device if sliced else per_device_general
        return jax.shard_map(
            body,
            mesh=mesh,
            in_specs=(P("dp", "seq", None), P(None, "dp", None), P(None, "dp"), P("dp", "seq", None)),
            out_specs=(P("dp", "seq", None), P("dp", "seq", None)),
            check_vma=False,
        )(signal, tap, out, cot)

    return run
```

```python
import functools
import jax
import jax.numpy as jnp
from jax import lax
from jax.experimental import pallas as pl
from jax.experimental.pallas import tpu as pltpu
from jax.sharding import PartitionSpec as P

DILATION_STEP = 32
PLANE = 8
F32 = jnp.float32
BF16 = jnp.bfloat16
ROOT = 0.7978845608028654
CUBIC = 0.044715


def gelu(v):
    return 0.5 * v * (1.0 + jnp.tanh(ROOT * (v + CUBIC * (v * v * v))))


def gelu_slope(v):
    square = v * v
    t = jnp.tanh(ROOT * v * (1.0 + CUBIC * square))
    return 0.5 * (1.0 + t) + (0.5 * ROOT) * v * (1.0 - t * t) * (1.0 + 3.0 * CUBIC * square)


def flip(index, bit):
    return index + bit - 2 * bit * ((index // bit) % 2)


def halo(block, width):
    count = lax.axis_size("seq")
    forward = [(i, i + 1) for i in range(count - 1)]
    backward = [(target, source) for source, target in forward]
    low = lax.ppermute(block[:, -width:], "seq", forward)
    high = lax.ppermute(block[:, :width], "seq", backward)
    return low, high


def plane_pairs(count, bit_even, bit_odd):
    return [(i, i ^ (bit_odd if i % 2 else bit_even)) for i in range(count)]


def slot_columns(slot, width):
    z = lax.axis_index("dp")
    for bit in (1, 2):
        if slot & bit:
            z = flip(z, bit)
    return pl.ds(pl.multiple_of(z * width, 128), width)


def held(name):
    s = lax.axis_index("seq") % PLANE

    def moved(index, step):
        return index + step - 2 * step * ((index // step) % 2)

    mine, mate = s, flip(s, 1)
    first, second = 2 + 2 * (s % 2), 4 - 2 * (s % 2)
    if name.startswith("mate_"):
        mine, first, second = mate, second, first
    name = name.removeprefix("mate_")
    if name in ("first", "last"):
        return [(matrix, mine % 2, None) for matrix in ((1,) if name == "first" else (2, 3))]
    pair = (mine, moved(mine, first)) if name == "near" else (moved(mine, second), flip(flip(mine, 2), 4))
    return [(q // 2, mine % 2, q) for q in pair]


def prepare_kernel(tap, out, piece, first, stage, sem, sems):
    s = lax.axis_index("seq") % PLANE
    matrix, half = s // 2, s % 2
    size = piece.shape[0]
    part = pl.ds(pl.multiple_of(half * size, 128), size)
    eighth = pl.ds(pl.multiple_of(s * (size // PLANE), 16), size // PLANE)
    copies = [
        (tap.at[1, :, part], first.at[0, 0:size]),
        (tap.at[0, eighth, 0:size], first.at[0, pl.ds(size, size // PLANE)]),
        (tap.at[0, eighth, size : 2 * size], first.at[0, pl.ds(size + size // PLANE, size // PLANE)]),
    ]
    copies = [pltpu.make_async_copy(a, b, sems.at[n]) for n, (a, b) in enumerate(copies)]

    @pl.when(matrix < 3)
    def _():
        copy = pltpu.make_async_copy(tap.at[matrix, :, part], piece, sem)
        copy.start()
        for other in copies:
            other.start()
        copy.wait()

    @pl.when(matrix == 3)
    def _():
        copy = pltpu.make_async_copy(out.at[part, :], stage, sem)
        copy.start()
        for other in copies:
            other.start()
        copy.wait()
        piece[...] = stage[...].T

    for other in copies:
        other.wait()


def bins_kernel(signal, cot, after, to_next, to_previous, sems):
    rows = signal.shape[1]
    step = DILATION_STEP
    copies = [
        (signal.at[:, rows - 2 * step :], to_next.at[:, 0 : 2 * step]),
        (cot.at[:, rows - step :], to_next.at[:, 2 * step :]),
        (cot.at[:, 0:step], to_previous.at[:, 0:step]),
        (signal.at[:, 0 : 2 * step], to_previous.at[:, step:]),
    ]
    copies = [pltpu.make_async_copy(a, b, sems.at[n]) for n, (a, b) in enumerate(copies)]
    for copy in copies:
        copy.start()
    for copy in copies:
        copy.wait()


def half_kernel(tap, out, last, stage, sems):
    half = lax.axis_index("seq") % 2
    size = last.shape[1]
    part = pl.ds(pl.multiple_of(half * size, 128), size)
    copies = [(out.at[part, :], stage), (tap.at[2, :, part], last.at[0])]
    copies = [pltpu.make_async_copy(a, b, sems.at[n]) for n, (a, b) in enumerate(copies)]
    for copy in copies:
        copy.start()
    copies[0].wait()
    last[1] = stage[...].T
    copies[1].wait()


def left_kernel(signal, cot, left, slope):
    reach = 2 * DILATION_STEP
    windows, rows, _ = signal.shape
    for w in range(windows):
        wide = signal[w].astype(F32)
        square = wide * wide
        t = jnp.tanh(ROOT * wide * (1.0 + CUBIC * square))
        left[0, w, reach : reach + rows] = (0.5 * wide * (1.0 + t)).astype(BF16)
        slope[w] = 0.5 * (1.0 + t) + (0.5 * ROOT) * wide * (1.0 - t * t) * (1.0 + 3.0 * CUBIC * square)
        left[1, w, DILATION_STEP : DILATION_STEP + rows] = cot[w]
        left[1, w, reach + rows :] = jnp.zeros_like(left[1, w, reach + rows :])


def pair_kernel(first, second, both, sems):
    copies = [pltpu.make_async_copy(a, both.at[n], sems.at[n]) for n, a in enumerate((first, second))]
    for copy in copies:
        copy.start()
    for copy in copies:
        copy.wait()


def join_kernel(piece, first, both, sems):
    size = piece.shape[0]
    copies = [(piece, both.at[0:size]), (first.at[0, size:], both.at[size:])]
    copies = [pltpu.make_async_copy(a, b, sems.at[n]) for n, (a, b) in enumerate(copies)]
    for copy in copies:
        copy.start()
    for copy in copies:
        copy.wait()


def edge_kernel(low, high, left_in, left, sems):
    reach = 2 * DILATION_STEP
    windows = low.shape[0]
    rows = left.shape[2] - 2 * reach
    copies = [
        (low.at[:, reach:], left.at[1, :, 0:DILATION_STEP]),
        (high.at[:, 0:DILATION_STEP], left.at[1, :, DILATION_STEP + rows : reach + rows]),
    ]
    copies = [pltpu.make_async_copy(a, b, sems.at[n]) for n, (a, b) in enumerate(copies)]
    for copy in copies:
        copy.start()
    for w in range(windows):
        left[0, w, 0:reach] = gelu(low[w, 0:reach].astype(F32)).astype(BF16)
        left[0, w, reach + rows :] = gelu(high[w, DILATION_STEP:].astype(F32)).astype(BF16)
    for copy in copies:
        copy.wait()


def rows_of(left, which, offset, rows, columns):
    return jnp.concatenate([left[which, w, pl.ds(offset, rows), columns] for w in range(left.shape[1])], axis=0)


LAST = (((1,), (1,)), ((), ()))


def own_kernel(left, tap, out, *sums):
    sums, out_t = sums[:2], sums[2]
    out_t[...] = out[...].T
    rows = left.shape[2] - 2 * DILATION_STEP
    size = tap.shape[1]
    columns = slot_columns(0, size)
    core = lax.axis_index("seq") % 2
    for side, half in zip(sums, (core, 1 - core)):
        part = pl.ds(pl.multiple_of(half * size, 128), size)
        inner = None
        for k in range(3):
            lhs = rows_of(left, 0, k * DILATION_STEP, rows, columns)
            term = jnp.dot(lhs, tap[k, :, part], preferred_element_type=F32)
            inner = term if inner is None else inner + term
        side[0] = inner
        lhs = rows_of(left, 1, 0, rows, columns)
        side[1] = lax.dot_general(lhs, out[part, :], LAST, preferred_element_type=F32)


def slot_kernel(slot, names, sides, fresh, carries, *refs):
    count = len(names)
    left, refs = refs[0], refs[1:]
    sums_in, refs = refs[:sides], refs[sides:]
    buffers, refs = refs[:count], refs[count:]
    refs = refs[0 if fresh else (2 if carries else 1) :]
    sums, whole, sems = refs[:sides], refs[sides], refs[-1]
    rows = left.shape[2] - 2 * DILATION_STEP
    size = buffers[0].shape[2]
    eighth = size // PLANE
    columns = slot_columns(slot, size)
    copies = []
    for buffer, name in zip(buffers, names):
        for i, (matrix, half, q) in enumerate(held(name)):
            part = pl.ds(pl.multiple_of(half * size, 128), size)
            copies.append((buffer.at[i, 0:size], whole.at[matrix, :, part]))
            if carries:
                at = pl.ds(pl.multiple_of(q * eighth, 16), eighth)
                for h in range(2):
                    source = buffer.at[i, pl.ds(size + h * eighth, eighth)]
                    copies.append((source, refs[sides + 1].at[at, pl.ds(h * size, size)]))
    copies = [pltpu.make_async_copy(a, b, sems.at[n]) for n, (a, b) in enumerate(copies)]
    for copy in copies:
        copy.start()
    for n, (side_in, side) in enumerate(zip(sums_in, sums)):
        totals = [side_in[0], side_in[1]]
        for buffer, name in zip(buffers, names):
            if sides == 2 and name.startswith("mate_") != (n == 1):
                continue
            for i, (matrix, _, _) in enumerate(held(name)):
                offset = (matrix % 3) * DILATION_STEP
                if not isinstance(matrix, int):
                    offset = pl.multiple_of(offset, DILATION_STEP)
                lhs = rows_of(left, matrix // 3, offset, rows, columns)
                term = jnp.dot(lhs, buffer[i, 0:size], preferred_element_type=F32)
                for which in range(2):
                    if not isinstance(matrix, int):
                        totals[which] = totals[which] + jnp.where(matrix // 3 == which, term, 0.0)
                    elif matrix // 3 == which:
                        totals[which] = totals[which] + term
        side[0], side[1] = totals
    for copy in copies:
        copy.wait()


def end_kernel(left, own, mate, buffer, pair_tap, whole_in, right, whole, sems):
    windows, rows = right.shape[1:3]
    size = buffer.shape[2]
    core = lax.axis_index("seq") % 2
    pieces = held("mate_far")
    copies = []
    for i, (matrix, half, _) in enumerate(pieces):
        part = pl.ds(pl.multiple_of(half * size, 128), size)
        copies.append(pltpu.make_async_copy(buffer.at[i], whole.at[matrix, :, part], sems.at[i]))
        copies[-1].start()
    lhs = rows_of(left, 0, 0, rows, slot_columns(1, size))
    for sums, half in ((own, core), (mate, 1 - core)):
        part = pl.ds(pl.multiple_of(half * size, 128), size)
        totals = [sums[0] + jnp.dot(lhs, pair_tap[:, part], preferred_element_type=F32), sums[1]]
        if sums is mate:
            for i, (matrix, _, _) in enumerate(pieces):
                offset = pl.multiple_of((matrix % 3) * DILATION_STEP, DILATION_STEP)
                mine = rows_of(left, matrix // 3, offset, rows, slot_columns(3, size))
                term = jnp.dot(mine, buffer[i], preferred_element_type=F32)
                for which in range(2):
                    totals[which] = totals[which] + jnp.where(matrix // 3 == which, term, 0.0)
        v = totals[0]
        square = v * v
        t = jnp.tanh(ROOT * v * (1.0 + CUBIC * square))
        slope = 0.5 * (1.0 + t) + (0.5 * ROOT) * v * (1.0 - t * t) * (1.0 + 3.0 * CUBIC * square)
        right[0, :, :, part] = (totals[1] * slope).astype(BF16).reshape(windows, rows, size)
        active = (0.5 * v * (1.0 + t)).astype(BF16).reshape(windows, rows, size)
        right[1, :, 2 * DILATION_STEP :, part] = active[:, DILATION_STEP : rows - DILATION_STEP]
    for copy in copies:
        copy.wait()


def back_kernel(signal, cot, slope, right, tap, out_t, pair_tap, *refs):
    wholes, (result, grad), (result_part, grad_part, sems) = refs[:3], refs[3:5], refs[5:]
    windows, rows, _ = signal.shape
    width = tap.shape[1]
    step = DILATION_STEP
    everything = slice(None)
    shifted = [rows_of(right, 0, (2 - k) * step, rows, everything) for k in range(3)]
    active = rows_of(right, 1, 2 * step, rows, everything)

    def matrix(slot, k):
        if slot == 0:
            return tap[k] if k < 3 else out_t[...]
        return pair_tap[...] if (slot, k) == (1, 0) else wholes[slot - 1][k]

    copies = []
    for slots in ((0, 1), (2, 3)):
        total = None
        for k in range(4):
            both = jnp.concatenate([matrix(slot, k) for slot in slots], axis=0)
            term = lax.dot_general(shifted[k] if k < 3 else active, both, LAST, preferred_element_type=F32)
            if k == 3:
                more = term
            else:
                total = term if total is None else total + term
        for n, slot in enumerate(slots):
            columns = slot_columns(slot, width)
            here = slice(n * width, (n + 1) * width)
            for w in range(windows):
                at = slice(w * rows, (w + 1) * rows)
                change = total[at, here] * slope[w, :, columns]
                grad_part[w, :, columns] = (cot[w, :, columns].astype(F32) + change).astype(BF16)
                result_part[w, :, columns] = (signal[w, :, columns].astype(F32) + more[at, here]).astype(BF16)
            for m, (part, whole) in enumerate(((result_part, result), (grad_part, grad))):
                copy = pltpu.make_async_copy(part.at[:, :, columns], whole.at[:, :, columns], sems.at[2 * slot + m])
                copy.start()
                copies.append(copy)
    for copy in copies:
        copy.wait()


def cost(microseconds):
    return pl.CostEstimate(flops=1000, bytes_accessed=1000, transcendentals=0)


def params(mib):
    return pltpu.CompilerParams(vmem_limit_bytes=mib << 20)


def tie(*values):
    return lax.optimization_barrier(values)


def per_device(signal, tap, out, cot):
    windows, rows, channels = signal.shape
    hidden = tap.shape[2]
    width = tap.shape[1]
    wide_rows = rows + 2 * DILATION_STEP
    vmem = pl.BlockSpec(memory_space=pltpu.VMEM)
    hbm = pl.BlockSpec(memory_space=pl.ANY)
    count = lax.axis_size("seq")

    def stay(array):
        return pltpu.with_memory_space_constraint(array, pltpu.HBM)

    reach = 2 * DILATION_STEP
    edge = jax.ShapeDtypeStruct((windows, reach + DILATION_STEP, channels), BF16)
    mine, first = pl.pallas_call(
        prepare_kernel,
        out_shape=[
            jax.ShapeDtypeStruct((width, width), BF16),
            jax.ShapeDtypeStruct((1, width + 2 * (width // PLANE), width), BF16),
        ],
        in_specs=[hbm] * 2,
        out_specs=[vmem] * 2,
        scratch_shapes=[
            pltpu.VMEM((width, width), BF16),
            pltpu.SemaphoreType.DMA,
            pltpu.SemaphoreType.DMA((3,)),
        ],
        compiler_params=params(8),
    )(stay(tap), stay(out))
    low, high = pl.pallas_call(
        bins_kernel,
        out_shape=[edge, edge],
        in_specs=[hbm] * 3,
        out_specs=[vmem] * 2,
        scratch_shapes=[pltpu.SemaphoreType.DMA((4,))],
        compiler_params=params(4),
    )(stay(signal), stay(cot), mine)

    def across(block, even, odd):
        return lax.ppermute(block, "seq", plane_pairs(count, even, odd))

    def over(block, bits):
        return lax.ppermute(block, "dp", [(i, i ^ bits) for i in range(4)])

    def moved_by(kernel, shape, *given):
        return pl.pallas_call(
            kernel,
            out_shape=jax.ShapeDtypeStruct(shape, BF16),
            in_specs=[hbm] * 2,
            out_specs=vmem,
            scratch_shapes=[pltpu.SemaphoreType.DMA((2,))],
            compiler_params=params(2),
            cost_estimate=cost(0.3),
        )(*given)

    def pair(first, second):
        return moved_by(pair_kernel, (2, *first.shape), first, second)

    side_shape = jax.ShapeDtypeStruct((2, windows * wide_rows, width), F32)
    whole_shape = jax.ShapeDtypeStruct((4, width, hidden), BF16)
    tap_shape = jax.ShapeDtypeStruct((width, hidden), BF16)

    def add_slot(slot, names, buffers, left, sums, *wholes, carries=False):
        given = [left, *sums, *buffers, *wholes]
        sides = len(sums)
        aliases = {1 + n: n for n in range(sides)}
        for n in range(len(wholes)):
            aliases[1 + sides + len(buffers) + n] = sides + n
        shapes = [side_shape] * sides + [whole_shape] + [tap_shape] * carries
        copies = sum(b.shape[0] for b in buffers) * (3 if carries else 1)
        done = pl.pallas_call(
            functools.partial(slot_kernel, slot, names, sides, not wholes, carries),
            out_shape=shapes,
            in_specs=[vmem] * (1 + sides + len(buffers)) + [hbm] * len(wholes),
            out_specs=[vmem] * sides + [hbm] * (1 + carries),
            scratch_shapes=[pltpu.SemaphoreType.DMA((copies,))],
            input_output_aliases=aliases,
            compiler_params=params(4),
            cost_estimate=cost(0.7 * len(names)),
        )(*given)
        return done[:sides], *done[sides:]

    p2 = over(mine, 2)
    first = over(first, 1)
    low = lax.ppermute(low, "seq", [(i, i + 1) for i in range(count - 1)])
    high = lax.ppermute(high, "seq", [(i + 1, i) for i in range(count - 1)])
    left_shape = jax.ShapeDtypeStruct((2, windows, rows + 2 * reach, channels), BF16)
    left, slope = pl.pallas_call(
        left_kernel,
        out_shape=[left_shape, jax.ShapeDtypeStruct(signal.shape, F32)],
        in_specs=[vmem] * 2,
        out_specs=[vmem] * 2,
        compiler_params=params(4),
        cost_estimate=cost(1.3),
    )(signal, cot)
    last = pl.pallas_call(
        half_kernel,
        out_shape=jax.ShapeDtypeStruct((2, width, width), BF16),
        in_specs=[hbm] * 2,
        out_specs=vmem,
        scratch_shapes=[pltpu.VMEM((width, width), BF16), pltpu.SemaphoreType.DMA((2,))],
        compiler_params=params(4),
        cost_estimate=cost(1.5),
    )(stay(tap), stay(out))
    p2, first, left, last = tie(p2, first, left, last)
    p3 = over(p2, 1)
    got2 = moved_by(join_kernel, (first.shape[1], width), p2, first)
    near2 = across(got2, 2, 4)
    left = pl.pallas_call(
        edge_kernel,
        out_shape=left_shape,
        in_specs=[vmem] * 3,
        out_specs=vmem,
        scratch_shapes=[pltpu.SemaphoreType.DMA((2,))],
        input_output_aliases={2: 0},
        compiler_params=params(4),
        cost_estimate=cost(0.5),
    )(low, high, left)
    *sums, out_t = pl.pallas_call(
        own_kernel,
        out_shape=[side_shape] * 2 + [tap_shape],
        in_specs=[vmem] * 3,
        out_specs=[vmem] * 3,
        compiler_params=params(4),
        cost_estimate=cost(1.4),
    )(left, tap, out)
    near_names, far_names = ("near", "mate_near"), ("far", "mate_far")
    mate_first = across(first, 1, 1)
    own2 = pair(got2, near2)
    own2, left = tie(own2, left)
    far2 = across(own2, 4, 2)
    mate2 = across(own2, 1, 1)
    p3, last, _, _ = tie(p3, last, low, high)
    near3 = across(p3, 2, 4)
    last = over(last, 1)
    far_mate2 = across(far2, 1, 1)
    sums, whole1 = add_slot(1, ("first", "mate_first"), (first, mate_first), left, sums)
    near3, *sums = tie(near3, *sums)
    own3 = pair(p3, near3)
    far3 = across(own3, 4, 2)
    mate3 = across(own3, 1, 1)
    mate_last = across(last, 1, 1)
    sums, whole2, pair_tap = add_slot(2, near_names, (own2, mate2), left, sums, carries=True)
    sums, whole3 = add_slot(3, near_names, (own3, mate3), left, sums)
    (own_sums,), whole2, pair_tap = add_slot(
        2, ("far",), (far2,), left, sums[:1], whole2, pair_tap, carries=True
    )
    sums = [own_sums, sums[1]]
    far3, mate_last, *sums = tie(far3, mate_last, *sums)
    (own_sums,), whole3 = add_slot(3, ("far",), (far3,), left, sums[:1], whole3)
    far3, own_sums = tie(far3, own_sums)
    far_mate3 = across(far3, 1, 1)
    sums = [own_sums, sums[1]]
    sums, whole1 = add_slot(1, ("last", "mate_last"), (last, mate_last), left, sums, whole1)
    (mate_sums,), whole2, pair_tap = add_slot(
        2, ("mate_far",), (far_mate2,), left, sums[1:], whole2, pair_tap, carries=True
    )
    sums = [sums[0], mate_sums]
    right, whole3 = pl.pallas_call(
        end_kernel,
        out_shape=[jax.ShapeDtypeStruct((2, windows, wide_rows, hidden), BF16), whole_shape],
        in_specs=[vmem] * 5 + [hbm],
        out_specs=[vmem, hbm],
        scratch_shapes=[pltpu.SemaphoreType.DMA((2,))],
        input_output_aliases={5: 1},
        compiler_params=params(4),
        cost_estimate=cost(1.6),
    )(left, sums[0], sums[1], far_mate3, pair_tap, whole3)
    result, grad_signal = pl.pallas_call(
        back_kernel,
        out_shape=[jax.ShapeDtypeStruct(signal.shape, BF16)] * 2,
        in_specs=[vmem] * 10,
        out_specs=[hbm] * 2,
        scratch_shapes=[pltpu.VMEM(signal.shape, BF16)] * 2 + [pltpu.SemaphoreType.DMA((8,))],
        compiler_params=params(8),
        cost_estimate=cost(4.5),
    )(signal, cot, slope, right, tap, out_t, pair_tap, whole1, whole2, whole3)
    return result, grad_signal


def extended(block, width):
    low, high = halo(block, width)
    return jnp.concatenate([low, block, high], axis=1)


def per_device_general(signal, tap, out, cot):
    tap = lax.all_gather(tap, "dp", axis=1, tiled=True)
    out = lax.all_gather(out, "dp", axis=1, tiled=True)
    rows = signal.shape[1]
    wide = signal.astype(F32)
    act = extended(gelu(wide).astype(BF16), DILATION_STEP)

    def contract(rule, a, b):
        return jnp.einsum(rule, a, b, preferred_element_type=F32)

    def window(block, k):
        return block[:, k * DILATION_STEP : k * DILATION_STEP + rows]

    inner = sum(contract("wtc,ch->wth", window(act, k), tap[k]) for k in range(3))
    active = gelu(inner).astype(BF16)
    result = wide + contract("wth,hc->wtc", active, out)
    grad_inner = (contract("wtc,hc->wth", cot, out) * gelu_slope(inner)).astype(BF16)
    grad_inner = extended(grad_inner, DILATION_STEP)
    grad_act = sum(contract("wth,ch->wtc", window(grad_inner, 2 - k), tap[k]) for k in range(3))
    grad_signal = cot.astype(F32) + grad_act * gelu_slope(wide)
    return result.astype(BF16), grad_signal.astype(BF16)


def solution(mesh):
    dp, seq = mesh.shape["dp"], mesh.shape["seq"]

    def run(signal, tap, out, cot):
        width = tap.shape[1] // dp
        hidden = tap.shape[2]
        sliced = dp == 4 and seq % PLANE == 0 and width % 128 == 0 and 2 * width == hidden
        body = per_device if sliced else per_device_general
        return jax.shard_map(
            body,
            mesh=mesh,
            in_specs=(P("dp", "seq", None), P(None, "dp", None), P(None, "dp"), P("dp", "seq", None)),
            out_specs=(P("dp", "seq", None), P("dp", "seq", None)),
            check_vma=False,
        )(signal, tap, out, cot)

    return run
```

```python
import functools
import jax
import jax.numpy as jnp
from jax import lax
from jax.experimental import pallas as pl
from jax.experimental.pallas import tpu as pltpu
from jax.sharding import PartitionSpec as P

DILATION_STEP = 32
PLANE = 8
F32 = jnp.float32
BF16 = jnp.bfloat16
ROOT = 0.7978845608028654
CUBIC = 0.044715


def gelu(v):
    return 0.5 * v * (1.0 + jnp.tanh(ROOT * (v + CUBIC * (v * v * v))))


def gelu_slope(v):
    square = v * v
    t = jnp.tanh(ROOT * v * (1.0 + CUBIC * square))
    return 0.5 * (1.0 + t) + (0.5 * ROOT) * v * (1.0 - t * t) * (1.0 + 3.0 * CUBIC * square)


def flip(index, bit):
    return index + bit - 2 * bit * ((index // bit) % 2)


def halo(block, width):
    count = lax.axis_size("seq")
    forward = [(i, i + 1) for i in range(count - 1)]
    backward = [(target, source) for source, target in forward]
    low = lax.ppermute(block[:, -width:], "seq", forward)
    high = lax.ppermute(block[:, :width], "seq", backward)
    return low, high


def plane_pairs(count, bit_even, bit_odd):
    return [(i, i ^ (bit_odd if i % 2 else bit_even)) for i in range(count)]


def slot_columns(slot, width):
    z = lax.axis_index("dp")
    for bit in (1, 2):
        if slot & bit:
            z = flip(z, bit)
    return pl.ds(pl.multiple_of(z * width, 128), width)


def held(name):
    s = lax.axis_index("seq") % PLANE

    def moved(index, step):
        return index + step - 2 * step * ((index // step) % 2)

    mine, mate = s, flip(s, 1)
    first, second = 2 + 2 * (s % 2), 4 - 2 * (s % 2)
    if name.startswith("mate_"):
        mine, first, second = mate, second, first
    name = name.removeprefix("mate_")
    if name in ("first", "last"):
        return [(matrix, mine % 2, None) for matrix in ((1,) if name == "first" else (2, 3))]
    pair = (mine, moved(mine, first)) if name == "near" else (moved(mine, second), flip(flip(mine, 2), 4))
    return [(q // 2, mine % 2, q) for q in pair]


def prepare_kernel(tap, out, piece, first, stage, sem, sems):
    s = lax.axis_index("seq") % PLANE
    matrix, half = s // 2, s % 2
    size = piece.shape[0]
    part = pl.ds(pl.multiple_of(half * size, 128), size)
    eighth = pl.ds(pl.multiple_of(s * (size // PLANE), 16), size // PLANE)
    copies = [
        (tap.at[1, :, part], first.at[0, 0:size]),
        (tap.at[0, eighth, 0:size], first.at[0, pl.ds(size, size // PLANE)]),
        (tap.at[0, eighth, size : 2 * size], first.at[0, pl.ds(size + size // PLANE, size // PLANE)]),
    ]
    copies = [pltpu.make_async_copy(a, b, sems.at[n]) for n, (a, b) in enumerate(copies)]

    @pl.when(matrix < 3)
    def _():
        copy = pltpu.make_async_copy(tap.at[matrix, :, part], piece, sem)
        copy.start()
        for other in copies:
            other.start()
        copy.wait()

    @pl.when(matrix == 3)
    def _():
        copy = pltpu.make_async_copy(out.at[part, :], stage, sem)
        copy.start()
        for other in copies:
            other.start()
        copy.wait()
        piece[...] = stage[...].T

    for other in copies:
        other.wait()


def bins_kernel(signal, cot, after, to_next, to_previous, sems):
    rows = signal.shape[1]
    step = DILATION_STEP
    copies = [
        (signal.at[:, rows - 2 * step :], to_next.at[:, 0 : 2 * step]),
        (cot.at[:, rows - step :], to_next.at[:, 2 * step :]),
        (cot.at[:, 0:step], to_previous.at[:, 0:step]),
        (signal.at[:, 0 : 2 * step], to_previous.at[:, step:]),
    ]
    copies = [pltpu.make_async_copy(a, b, sems.at[n]) for n, (a, b) in enumerate(copies)]
    for copy in copies:
        copy.start()
    for copy in copies:
        copy.wait()


def half_kernel(tap, out, last, stage, sems):
    half = lax.axis_index("seq") % 2
    size = last.shape[1]
    part = pl.ds(pl.multiple_of(half * size, 128), size)
    copies = [(out.at[part, :], stage), (tap.at[2, :, part], last.at[0])]
    copies = [pltpu.make_async_copy(a, b, sems.at[n]) for n, (a, b) in enumerate(copies)]
    for copy in copies:
        copy.start()
    copies[0].wait()
    last[1] = stage[...].T
    copies[1].wait()


def left_kernel(signal, cot, left, slope):
    reach = 2 * DILATION_STEP
    windows, rows, _ = signal.shape
    for w in range(windows):
        wide = signal[w].astype(F32)
        square = wide * wide
        t = jnp.tanh(ROOT * wide * (1.0 + CUBIC * square))
        left[0, w, reach : reach + rows] = (0.5 * wide * (1.0 + t)).astype(BF16)
        slope[w] = 0.5 * (1.0 + t) + (0.5 * ROOT) * wide * (1.0 - t * t) * (1.0 + 3.0 * CUBIC * square)
        left[1, w, DILATION_STEP : DILATION_STEP + rows] = cot[w]
        left[1, w, reach + rows :] = jnp.zeros_like(left[1, w, reach + rows :])


def pair_kernel(first, second, both, sems):
    copies = [pltpu.make_async_copy(a, both.at[n], sems.at[n]) for n, a in enumerate((first, second))]
    for copy in copies:
        copy.start()
    for copy in copies:
        copy.wait()


def join_kernel(piece, first, both, sems):
    size = piece.shape[0]
    copies = [(piece, both.at[0:size]), (first.at[0, size:], both.at[size:])]
    copies = [pltpu.make_async_copy(a, b, sems.at[n]) for n, (a, b) in enumerate(copies)]
    for copy in copies:
        copy.start()
    for copy in copies:
        copy.wait()


def edge_kernel(low, high, left_in, left, sems):
    reach = 2 * DILATION_STEP
    windows = low.shape[0]
    rows = left.shape[2] - 2 * reach
    copies = [
        (low.at[:, reach:], left.at[1, :, 0:DILATION_STEP]),
        (high.at[:, 0:DILATION_STEP], left.at[1, :, DILATION_STEP + rows : reach + rows]),
    ]
    copies = [pltpu.make_async_copy(a, b, sems.at[n]) for n, (a, b) in enumerate(copies)]
    for copy in copies:
        copy.start()
    for w in range(windows):
        left[0, w, 0:reach] = gelu(low[w, 0:reach].astype(F32)).astype(BF16)
        left[0, w, reach + rows :] = gelu(high[w, DILATION_STEP:].astype(F32)).astype(BF16)
    for copy in copies:
        copy.wait()


def rows_of(left, which, offset, rows, columns):
    return jnp.concatenate([left[which, w, pl.ds(offset, rows), columns] for w in range(left.shape[1])], axis=0)


LAST = (((1,), (1,)), ((), ()))


def own_kernel(left, tap, out, *sums):
    sums, out_t = sums[:2], sums[2]
    out_t[...] = out[...].T
    rows = left.shape[2] - 2 * DILATION_STEP
    size = tap.shape[1]
    columns = slot_columns(0, size)
    core = lax.axis_index("seq") % 2
    for side, half in zip(sums, (core, 1 - core)):
        part = pl.ds(pl.multiple_of(half * size, 128), size)
        inner = None
        for k in range(3):
            lhs = rows_of(left, 0, k * DILATION_STEP, rows, columns)
            term = jnp.dot(lhs, tap[k, :, part], preferred_element_type=F32)
            inner = term if inner is None else inner + term
        side[0] = inner
        lhs = rows_of(left, 1, 0, rows, columns)
        side[1] = lax.dot_general(lhs, out[part, :], LAST, preferred_element_type=F32)


def slot_kernel(slot, names, sides, fresh, carries, *refs):
    count = len(names)
    left, refs = refs[0], refs[1:]
    sums_in, refs = refs[:sides], refs[sides:]
    buffers, refs = refs[:count], refs[count:]
    refs = refs[0 if fresh else (2 if carries else 1) :]
    sums, whole, sems = refs[:sides], refs[sides], refs[-1]
    rows = left.shape[2] - 2 * DILATION_STEP
    size = buffers[0].shape[2]
    eighth = size // PLANE
    columns = slot_columns(slot, size)
    copies = []
    for buffer, name in zip(buffers, names):
        for i, (matrix, half, q) in enumerate(held(name)):
            part = pl.ds(pl.multiple_of(half * size, 128), size)
            copies.append((buffer.at[i, 0:size], whole.at[matrix, :, part]))
            if carries:
                at = pl.ds(pl.multiple_of(q * eighth, 16), eighth)
                for h in range(2):
                    source = buffer.at[i, pl.ds(size + h * eighth, eighth)]
                    copies.append((source, refs[sides + 1].at[at, pl.ds(h * size, size)]))
    copies = [pltpu.make_async_copy(a, b, sems.at[n]) for n, (a, b) in enumerate(copies)]
    for copy in copies:
        copy.start()
    for n, (side_in, side) in enumerate(zip(sums_in, sums)):
        totals = [side_in[0], side_in[1]]
        for buffer, name in zip(buffers, names):
            if sides == 2 and name.startswith("mate_") != (n == 1):
                continue
            for i, (matrix, _, _) in enumerate(held(name)):
                offset = (matrix % 3) * DILATION_STEP
                if not isinstance(matrix, int):
                    offset = pl.multiple_of(offset, DILATION_STEP)
                lhs = rows_of(left, matrix // 3, offset, rows, columns)
                term = jnp.dot(lhs, buffer[i, 0:size], preferred_element_type=F32)
                for which in range(2):
                    if not isinstance(matrix, int):
                        totals[which] = totals[which] + jnp.where(matrix // 3 == which, term, 0.0)
                    elif matrix // 3 == which:
                        totals[which] = totals[which] + term
        side[0], side[1] = totals
    for copy in copies:
        copy.wait()


def end_kernel(left, own, mate, buffer, pair_tap, whole_in, right, whole, sems):
    windows, rows = right.shape[1:3]
    size = buffer.shape[2]
    core = lax.axis_index("seq") % 2
    pieces = held("mate_far")
    copies = []
    for i, (matrix, half, _) in enumerate(pieces):
        part = pl.ds(pl.multiple_of(half * size, 128), size)
        copies.append(pltpu.make_async_copy(buffer.at[i], whole.at[matrix, :, part], sems.at[i]))
        copies[-1].start()
    lhs = rows_of(left, 0, 0, rows, slot_columns(1, size))
    for sums, half in ((own, core), (mate, 1 - core)):
        part = pl.ds(pl.multiple_of(half * size, 128), size)
        totals = [sums[0] + jnp.dot(lhs, pair_tap[:, part], preferred_element_type=F32), sums[1]]
        if sums is mate:
            for i, (matrix, _, _) in enumerate(pieces):
                offset = pl.multiple_of((matrix % 3) * DILATION_STEP, DILATION_STEP)
                mine = rows_of(left, matrix // 3, offset, rows, slot_columns(3, size))
                term = jnp.dot(mine, buffer[i], preferred_element_type=F32)
                for which in range(2):
                    totals[which] = totals[which] + jnp.where(matrix // 3 == which, term, 0.0)
        v = totals[0]
        square = v * v
        t = jnp.tanh(ROOT * v * (1.0 + CUBIC * square))
        slope = 0.5 * (1.0 + t) + (0.5 * ROOT) * v * (1.0 - t * t) * (1.0 + 3.0 * CUBIC * square)
        right[0, :, :, part] = (totals[1] * slope).astype(BF16).reshape(windows, rows, size)
        active = (0.5 * v * (1.0 + t)).astype(BF16).reshape(windows, rows, size)
        right[1, :, 2 * DILATION_STEP :, part] = active[:, DILATION_STEP : rows - DILATION_STEP]
    for copy in copies:
        copy.wait()


def back_kernel(signal, cot, slope, right, tap, out_t, pair_tap, *refs):
    wholes, (result, grad), (result_part, grad_part, sems) = refs[:3], refs[3:5], refs[5:]
    windows, rows, _ = signal.shape
    width = tap.shape[1]
    step = DILATION_STEP
    everything = slice(None)
    shifted = [rows_of(right, 0, (2 - k) * step, rows, everything) for k in range(3)]
    active = rows_of(right, 1, 2 * step, rows, everything)

    def matrix(slot, k):
        if slot == 0:
            return tap[k] if k < 3 else out_t[...]
        return pair_tap[...] if (slot, k) == (1, 0) else wholes[slot - 1][k]

    copies = []
    for slots in ((0, 1), (2, 3)):
        total = None
        for k in range(4):
            both = jnp.concatenate([matrix(slot, k) for slot in slots], axis=0)
            term = lax.dot_general(shifted[k] if k < 3 else active, both, LAST, preferred_element_type=F32)
            if k == 3:
                more = term
            else:
                total = term if total is None else total + term
        for n, slot in enumerate(slots):
            columns = slot_columns(slot, width)
            here = slice(n * width, (n + 1) * width)
            for w in range(windows):
                at = slice(w * rows, (w + 1) * rows)
                change = total[at, here] * slope[w, :, columns]
                grad_part[w, :, columns] = (cot[w, :, columns].astype(F32) + change).astype(BF16)
                result_part[w, :, columns] = (signal[w, :, columns].astype(F32) + more[at, here]).astype(BF16)
            for m, (part, whole) in enumerate(((result_part, result), (grad_part, grad))):
                copy = pltpu.make_async_copy(part.at[:, :, columns], whole.at[:, :, columns], sems.at[2 * slot + m])
                copy.start()
                copies.append(copy)
    for copy in copies:
        copy.wait()


def cost(microseconds):
    return pl.CostEstimate(flops=1000, bytes_accessed=1000, transcendentals=0)


def params(mib):
    return pltpu.CompilerParams(vmem_limit_bytes=mib << 20)


def tie(*values):
    return lax.optimization_barrier(values)


def per_device(signal, tap, out, cot):
    windows, rows, channels = signal.shape
    hidden = tap.shape[2]
    width = tap.shape[1]
    wide_rows = rows + 2 * DILATION_STEP
    vmem = pl.BlockSpec(memory_space=pltpu.VMEM)
    hbm = pl.BlockSpec(memory_space=pl.ANY)
    count = lax.axis_size("seq")

    def stay(array):
        return pltpu.with_memory_space_constraint(array, pltpu.HBM)

    reach = 2 * DILATION_STEP
    edge = jax.ShapeDtypeStruct((windows, reach + DILATION_STEP, channels), BF16)
    mine, first = pl.pallas_call(
        prepare_kernel,
        out_shape=[
            jax.ShapeDtypeStruct((width, width), BF16),
            jax.ShapeDtypeStruct((1, width + 2 * (width // PLANE), width), BF16),
        ],
        in_specs=[hbm] * 2,
        out_specs=[vmem] * 2,
        scratch_shapes=[
            pltpu.VMEM((width, width), BF16),
            pltpu.SemaphoreType.DMA,
            pltpu.SemaphoreType.DMA((3,)),
        ],
        compiler_params=params(8),
    )(stay(tap), stay(out))
    low, high = pl.pallas_call(
        bins_kernel,
        out_shape=[edge, edge],
        in_specs=[hbm] * 3,
        out_specs=[vmem] * 2,
        scratch_shapes=[pltpu.SemaphoreType.DMA((4,))],
        compiler_params=params(4),
    )(stay(signal), stay(cot), mine)

    def across(block, even, odd):
        return lax.ppermute(block, "seq", plane_pairs(count, even, odd))

    def over(block, bits):
        return lax.ppermute(block, "dp", [(i, i ^ bits) for i in range(4)])

    def moved_by(kernel, shape, *given):
        return pl.pallas_call(
            kernel,
            out_shape=jax.ShapeDtypeStruct(shape, BF16),
            in_specs=[hbm] * 2,
            out_specs=vmem,
            scratch_shapes=[pltpu.SemaphoreType.DMA((2,))],
            compiler_params=params(2),
            cost_estimate=cost(0.3),
        )(*given)

    def pair(first, second):
        return moved_by(pair_kernel, (2, *first.shape), first, second)

    side_shape = jax.ShapeDtypeStruct((2, windows * wide_rows, width), F32)
    whole_shape = jax.ShapeDtypeStruct((4, width, hidden), BF16)
    tap_shape = jax.ShapeDtypeStruct((width, hidden), BF16)

    def add_slot(slot, names, buffers, left, sums, *wholes, carries=False):
        given = [left, *sums, *buffers, *wholes]
        sides = len(sums)
        aliases = {1 + n: n for n in range(sides)}
        for n in range(len(wholes)):
            aliases[1 + sides + len(buffers) + n] = sides + n
        shapes = [side_shape] * sides + [whole_shape] + [tap_shape] * carries
        copies = sum(b.shape[0] for b in buffers) * (3 if carries else 1)
        done = pl.pallas_call(
            functools.partial(slot_kernel, slot, names, sides, not wholes, carries),
            out_shape=shapes,
            in_specs=[vmem] * (1 + sides + len(buffers)) + [hbm] * len(wholes),
            out_specs=[vmem] * sides + [hbm] * (1 + carries),
            scratch_shapes=[pltpu.SemaphoreType.DMA((copies,))],
            input_output_aliases=aliases,
            compiler_params=params(4),
            cost_estimate=cost(0.7 * len(names)),
        )(*given)
        return done[:sides], *done[sides:]

    p2 = over(mine, 2)
    first = over(first, 1)
    low = lax.ppermute(low, "seq", [(i, i + 1) for i in range(count - 1)])
    high = lax.ppermute(high, "seq", [(i + 1, i) for i in range(count - 1)])
    left_shape = jax.ShapeDtypeStruct((2, windows, rows + 2 * reach, channels), BF16)
    left, slope = pl.pallas_call(
        left_kernel,
        out_shape=[left_shape, jax.ShapeDtypeStruct(signal.shape, F32)],
        in_specs=[vmem] * 2,
        out_specs=[vmem] * 2,
        compiler_params=params(4),
        cost_estimate=cost(1.3),
    )(signal, cot)
    last = pl.pallas_call(
        half_kernel,
        out_shape=jax.ShapeDtypeStruct((2, width, width), BF16),
        in_specs=[hbm] * 2,
        out_specs=vmem,
        scratch_shapes=[pltpu.VMEM((width, width), BF16), pltpu.SemaphoreType.DMA((2,))],
        compiler_params=params(4),
        cost_estimate=cost(1.5),
    )(stay(tap), stay(out))
    p2, first, left, last = tie(p2, first, left, last)
    p3 = over(p2, 1)
    got2 = moved_by(join_kernel, (first.shape[1], width), p2, first)
    near2 = across(got2, 2, 4)
    left = pl.pallas_call(
        edge_kernel,
        out_shape=left_shape,
        in_specs=[vmem] * 3,
        out_specs=vmem,
        scratch_shapes=[pltpu.SemaphoreType.DMA((2,))],
        input_output_aliases={2: 0},
        compiler_params=params(4),
        cost_estimate=cost(0.5),
    )(low, high, left)
    *sums, out_t = pl.pallas_call(
        own_kernel,
        out_shape=[side_shape] * 2 + [tap_shape],
        in_specs=[vmem] * 3,
        out_specs=[vmem] * 3,
        compiler_params=params(4),
        cost_estimate=cost(1.4),
    )(left, tap, out)
    near_names, far_names = ("near", "mate_near"), ("far", "mate_far")
    mate_first = across(first, 1, 1)
    own2 = pair(got2, near2)
    own2, left = tie(own2, left)
    far2 = across(own2, 4, 2)
    mate2 = across(own2, 1, 1)
    p3, last, _, _ = tie(p3, last, low, high)
    near3 = across(p3, 2, 4)
    last = over(last, 1)
    far_mate2 = across(far2, 1, 1)
    sums, whole1 = add_slot(1, ("first", "mate_first"), (first, mate_first), left, sums)
    near3, *sums = tie(near3, *sums)
    own3 = pair(p3, near3)
    far3 = across(own3, 4, 2)
    mate3 = across(own3, 1, 1)
    mate_last = across(last, 1, 1)
    sums, whole2, pair_tap = add_slot(2, near_names, (own2, mate2), left, sums, carries=True)
    sums, whole3 = add_slot(3, near_names, (own3, mate3), left, sums)
    (own_sums,), whole2, pair_tap = add_slot(
        2, ("far",), (far2,), left, sums[:1], whole2, pair_tap, carries=True
    )
    sums = [own_sums, sums[1]]
    (own_sums,), whole1 = add_slot(1, ("last",), (last,), left, sums[:1], whole1)
    sums = [own_sums, sums[1]]
    far3, mate_last, *sums = tie(far3, mate_last, *sums)
    (own_sums,), whole3 = add_slot(3, ("far",), (far3,), left, sums[:1], whole3)
    far3, own_sums = tie(far3, own_sums)
    far_mate3 = across(far3, 1, 1)
    sums = [own_sums, sums[1]]
    (mate_sums,), whole1 = add_slot(1, ("mate_last",), (mate_last,), left, sums[1:], whole1)
    sums = [sums[0], mate_sums]
    (mate_sums,), whole2, pair_tap = add_slot(
        2, ("mate_far",), (far_mate2,), left, sums[1:], whole2, pair_tap, carries=True
    )
    sums = [sums[0], mate_sums]
    right, whole3 = pl.pallas_call(
        end_kernel,
        out_shape=[jax.ShapeDtypeStruct((2, windows, wide_rows, hidden), BF16), whole_shape],
        in_specs=[vmem] * 5 + [hbm],
        out_specs=[vmem, hbm],
        scratch_shapes=[pltpu.SemaphoreType.DMA((2,))],
        input_output_aliases={5: 1},
        compiler_params=params(4),
        cost_estimate=cost(1.6),
    )(left, sums[0], sums[1], far_mate3, pair_tap, whole3)
    result, grad_signal = pl.pallas_call(
        back_kernel,
        out_shape=[jax.ShapeDtypeStruct(signal.shape, BF16)] * 2,
        in_specs=[vmem] * 10,
        out_specs=[hbm] * 2,
        scratch_shapes=[pltpu.VMEM(signal.shape, BF16)] * 2 + [pltpu.SemaphoreType.DMA((8,))],
        compiler_params=params(8),
        cost_estimate=cost(4.5),
    )(signal, cot, slope, right, tap, out_t, pair_tap, whole1, whole2, whole3)
    return result, grad_signal


def extended(block, width):
    low, high = halo(block, width)
    return jnp.concatenate([low, block, high], axis=1)


def per_device_general(signal, tap, out, cot):
    tap = lax.all_gather(tap, "dp", axis=1, tiled=True)
    out = lax.all_gather(out, "dp", axis=1, tiled=True)
    rows = signal.shape[1]
    wide = signal.astype(F32)
    act = extended(gelu(wide).astype(BF16), DILATION_STEP)

    def contract(rule, a, b):
        return jnp.einsum(rule, a, b, preferred_element_type=F32)

    def window(block, k):
        return block[:, k * DILATION_STEP : k * DILATION_STEP + rows]

    inner = sum(contract("wtc,ch->wth", window(act, k), tap[k]) for k in range(3))
    active = gelu(inner).astype(BF16)
    result = wide + contract("wth,hc->wtc", active, out)
    grad_inner = (contract("wtc,hc->wth", cot, out) * gelu_slope(inner)).astype(BF16)
    grad_inner = extended(grad_inner, DILATION_STEP)
    grad_act = sum(contract("wth,ch->wtc", window(grad_inner, 2 - k), tap[k]) for k in range(3))
    grad_signal = cot.astype(F32) + grad_act * gelu_slope(wide)
    return result.astype(BF16), grad_signal.astype(BF16)


def solution(mesh):
    dp, seq = mesh.shape["dp"], mesh.shape["seq"]

    def run(signal, tap, out, cot):
        width = tap.shape[1] // dp
        hidden = tap.shape[2]
        sliced = dp == 4 and seq % PLANE == 0 and width % 128 == 0 and 2 * width == hidden
        body = per_device if sliced else per_device_general
        return jax.shard_map(
            body,
            mesh=mesh,
            in_specs=(P("dp", "seq", None), P(None, "dp", None), P(None, "dp"), P("dp", "seq", None)),
            out_specs=(P("dp", "seq", None), P("dp", "seq", None)),
            check_vma=False,
        )(signal, tap, out, cot)

    return run
```
